256 devices in a mesh: seq: 64 (over z, y, core), head: 4 (over x).
Axes of the slice: x: 4, y: 4, z: 8, core: 2. Of those that a mesh axis runs over, the one named last changes fastest.
Arguments:
- latents: bfloat16 [128, 256, 64], P('seq'), may hold values from -6 to 6
- clip_ids: int32 [128], P('seq'), may hold values from 0 to 31, never falling along the last dimension, each value on 1 to 8 neighbouring positions
- owners: int32 [128], P('seq'), may hold values from 0 to 63, as said below
- slots: int32 [128], P('seq'), may hold values from 0 to 3, as said below
- extents: int32 [32, 2], replicated, may hold values from 8 to 48
- embed_weight: bfloat16 [64, 3072], replicated, may hold values from -0.75 to 0.75
- embed_bias: float32 [3072], replicated, may hold values from -3 to 3
- shift_table: bfloat16 [32, 3072], replicated, may hold values from -3 to 3
- scale_table: bfloat16 [32, 3072], replicated, may hold values from -1.796875 to 1.796875
- query_weight: bfloat16 [3072, 3072], P(None, 'head'), may hold values from -0.109375 to 0.109375
- key_weight: bfloat16 [3072, 3072], P(None, 'head'), may hold values from -0.109375 to 0.109375
- query_gain: float32 [128], replicated, may hold values from 0.1 to 1.9
- key_gain: float32 [128], replicated, may hold values from 0.1 to 1.9
Outputs:
- query_out: bfloat16 [65536, 3072], P('seq', 'head')
- key_out: bfloat16 [65536, 3072], P('seq', 'head')
The draws below stay inside these ranges and needn't reach their ends.
Inputs may be any that keep to these rules, and one draw needn't show every extreme that they name: `clip_ids`: clip ids never fall along the blocks, and each clip has 1 to 8 blocks. The 2 blocks of one index of seq go to different owners; an owner receives at most 4 blocks, and some owner receives exactly 4. `slots`: no two blocks share both owner and slot.
All inputs are finite; a program needn't handle non-finite values.
Results may differ from the reference program's by a relative error of at most 0.0049.
Values may be sent and summed in bfloat16 or wider, within the bound.
A program may use at most 128 MiB of HBM per device.

```python
import math
import jax
import jax.numpy as jnp
import numpy as np
from jax import lax

D = 3072
PATCH_IN = 64
HEAD_DIM = 128
TOK_BLOCK = 256
MOST_BLK = 8
BLK_DEV = 2
RANKS = 64
OWN_SLOTS = 4
BLOCKS = 128
CLIPS = 32


def route_plan(key):
    base = jax.random.fold_in(key, 7)
    spacing = RANKS // BLK_DEV
    center = jax.random.randint(jax.random.fold_in(base, 1), (), 0, RANKS)
    halves = jnp.arange(2 * RANKS, dtype=jnp.int32)
    lanes = jnp.arange(BLK_DEV, dtype=jnp.int32)
    forced = jnp.any(halves[:, None] // 2 == (center - lanes[None, :] * spacing) % RANKS, axis=1)
    ranking = jax.random.permutation(jax.random.fold_in(base, 2), 2 * RANKS).astype(jnp.int32)
    scores = ranking - jnp.where(forced, 4 * RANKS, 0)
    chosen = jnp.argsort(scores, stable=True)[:RANKS].astype(jnp.int32)
    order = jax.random.permutation(jax.random.fold_in(base, 3), RANKS)
    assigned = chosen[order]
    owner_grid = (assigned[:, None] // 2 + lanes[None, :] * spacing) % RANKS
    slot_grid = 2 * lanes[None, :] + assigned[:, None] % 2
    return (owner_grid.reshape(-1).astype(jnp.int32), slot_grid.reshape(-1).astype(jnp.int32))


def draw_owners(key, part):
    return route_plan(key)[0]


def draw_slots(key, part):
    return route_plan(key)[1]


def place_ends(result, key, least, high):
    index_at = [jax.random.randint(jax.random.fold_in(key, axis), (), 0, length) for axis, length in enumerate(result.shape)]
    main_axis = result.shape.index(max(result.shape))
    beside = index_at[:main_axis] + [(index_at[main_axis] + 1) % result.shape[main_axis]] + index_at[main_axis + 1:]
    return result.at[tuple(index_at)].set(least).at[tuple(beside)].set(high)


def block_levels(own_key, dims, cuts, least, top_value):
    def one(dim, shards_of):
        steps = jax.random.uniform(jax.random.fold_in(jax.random.fold_in(own_key, 6), dim), (shards_of,), jnp.float32, least / len(cuts), top_value / len(cuts))
        return jnp.repeat(jnp.exp(steps), dims[dim] // shards_of).reshape((-1,) + (1,) * (len(dims) - dim - 1))

    gain = one(*cuts[0])
    for cut in cuts[1:]:
        gain = gain * one(*cut)
    return gain


def length_profile(amount, total, limit, slope):
    loads = [(1 << 20) // math.isqrt(rank ** slope) + 1 for rank in range(2, amount + 1)]
    rest, holding = total - limit - (amount - 1), [1] * (amount - 1)
    while rest > 0:
        candidates = [i for i in range(amount - 1) if holding[i] < limit]
        mass, budget = sum([loads[i] for i in candidates]), rest
        for i in candidates:
            more = min(limit - holding[i], max(1, budget * loads[i] // mass), rest)
            holding[i] = holding[i] + more
            rest = rest - more
    return np.array([limit] + holding)


def ragged_sizes(stream_key, number_of, total, most, skew):
    if number_of == 2:
        one = jax.random.randint(stream_key, (), max(1, total - most), min(most, total - 1) + 1)
        return jnp.stack([one, total - one])
    tallies = jnp.asarray(length_profile(number_of, total, most, skew), jnp.int32)
    pairs = (number_of - 1) // 2
    giver, receiver = tallies[1:1 + 2 * pairs:2], tallies[2:2 + 2 * pairs:2]
    room = jnp.minimum(giver - 1, most - receiver)
    passed = jax.random.randint(jax.random.fold_in(stream_key, 1), (pairs,), 0, 1 << 20) % (room + 1)
    tallies = tallies.at[1:1 + 2 * pairs:2].set(giver - passed).at[2:2 + 2 * pairs:2].set(receiver + passed)
    return tallies[jax.random.permutation(jax.random.fold_in(stream_key, 2), number_of)]


def scatter_about(key, shape, deviation, reach, cuts=(), kind=jnp.bfloat16):
    gain = block_levels(key, shape, cuts, -0.22, 0.18) if cuts else 1.0
    entries = jax.random.normal(key, shape, jnp.float32) * deviation * gain
    return jnp.minimum(jnp.maximum(entries, -reach), reach).astype(kind)


def setup_inputs(seed: int = 0) -> dict:
    key_of = jax.random.split(jax.random.key(seed), 14)
    latents = scatter_about(key_of[0], (BLOCKS, TOK_BLOCK, PATCH_IN), 1.0, 6.0, ((0, 64),))
    clip_ids = jnp.searchsorted(jnp.cumsum(ragged_sizes(key_of[1], CLIPS, BLOCKS, MOST_BLK, 1)), jnp.arange(BLOCKS), side="right").astype(jnp.int32)
    owners = draw_owners(jax.random.fold_in(key_of[13], 71), 0)
    slots = draw_slots(jax.random.fold_in(key_of[13], 71), 0)
    extents = place_ends(jax.random.randint(key_of[4], (CLIPS, 2), 8, 49), jax.random.fold_in(key_of[4], 1), 8, 48).astype(jnp.int32)
    embed_weight = scatter_about(key_of[5], (PATCH_IN, D), PATCH_IN ** -0.5, 0.75)
    embed_bias = scatter_about(key_of[6], (D,), 0.5, 3.0, (), jnp.float32)
    shift_table = scatter_about(key_of[7], (CLIPS, D), 0.5, 3.0)
    scale_table = scatter_about(key_of[8], (CLIPS, D), 0.3, 1.796875)
    query_weight = scatter_about(key_of[9], (D, D), D ** -0.5, 0.109375, ((1, 4),))
    key_weight = scatter_about(key_of[10], (D, D), D ** -0.5, 0.109375, ((1, 4),))
    query_gain = jnp.clip(1.0 + 0.18 * jax.random.normal(key_of[11], (HEAD_DIM,), jnp.float32), 0.1, 1.9)
    key_gain = jnp.clip(1.0 + 0.18 * jax.random.normal(key_of[12], (HEAD_DIM,), jnp.float32), 0.1, 1.9)
    return dict(latents=latents, clip_ids=clip_ids, owners=owners, slots=slots, extents=extents, embed_weight=embed_weight, embed_bias=embed_bias, shift_table=shift_table, scale_table=scale_table, query_weight=query_weight, key_weight=key_weight, query_gain=query_gain, key_gain=key_gain)


def token_angles(offsets, heights, widths, block_tokens):
    within = offsets[:, None] + jnp.arange(block_tokens, dtype=jnp.int32)[None, :]
    plane_size = heights * widths
    frames = within // plane_size[:, None]
    row_pos = within // widths[:, None] % heights[:, None]
    col_pos = within % widths[:, None]
    pieces = []
    for position, axis_width in ((frames, 16), (row_pos, 56), (col_pos, 56)):
        frequency = 1.0 / 10000.0 ** (jnp.arange(0, axis_width, 2, dtype=jnp.float32) / axis_width)
        pieces.append(position.reshape(-1).astype(jnp.float32)[:, None] * frequency[None, :])
    return jnp.concatenate(pieces, axis=1)

def finish(values, gains, angles):
    row_count, column_count = values.shape
    head_size = gains.shape[0]
    head_count = column_count // head_size
    grouped = values.reshape(row_count, head_count, head_size)
    inverse = lax.rsqrt(lax.optimization_barrier(jnp.mean(grouped * grouped, axis=2, keepdims=True)) + 1e-06)
    normed = grouped * inverse * gains
    paired = normed.reshape(row_count, head_count, head_size // 2, 2)
    even_part = paired[..., 0]
    odd_part = paired[..., 1]
    cosines = jnp.cos(angles)[:, None, :]
    sines = jnp.sin(angles)[:, None, :]
    turned = jnp.stack([even_part * cosines - odd_part * sines, even_part * sines + odd_part * cosines], axis=-1)
    return turned.reshape(row_count, column_count).astype(jnp.bfloat16)

def project(latent, shift_rows, scale_rows, angles, embed_weight, embed_bias, query_weight, key_weight, query_gain, key_gain):
    block_count, token_count, channels = latent.shape
    hidden = jnp.dot(latent.reshape(block_count * token_count, channels), embed_weight, preferred_element_type=jnp.float32) + embed_bias
    average = lax.optimization_barrier(jnp.mean(hidden, axis=1, keepdims=True))
    centred = hidden - average
    variance = lax.optimization_barrier(jnp.mean(centred * centred, axis=1, keepdims=True))
    normed = (centred * lax.rsqrt(variance + 1e-06)).reshape(block_count, token_count, -1)
    modulated = normed * (1.0 + scale_rows[:, None, :]) + shift_rows[:, None, :]
    modulated = modulated.astype(jnp.bfloat16).reshape(block_count * token_count, -1)
    queries = jnp.dot(modulated, query_weight, preferred_element_type=jnp.float32)
    key_rows = jnp.dot(modulated, key_weight, preferred_element_type=jnp.float32)
    return (finish(queries, query_gain, angles), finish(key_rows, key_gain, angles))

def reference(latents, clip_ids, owners, slots, extents, embed_weight, embed_bias, shift_table, scale_table, query_weight, key_weight, query_gain, key_gain):
    block_total, block_tokens, channels = latents.shape
    earlier = lax.optimization_barrier(jnp.sum((clip_ids[None, :] < clip_ids[:, None]).astype(jnp.int32), axis=1))
    offsets = (jnp.arange(block_total, dtype=jnp.int32) - earlier) * block_tokens

    def one_block(position):
        clip_index = clip_ids[position]
        angles = token_angles(offsets[position][None], extents[clip_index, 0][None], extents[clip_index, 1][None], block_tokens)
        latent = lax.dynamic_slice_in_dim(latents, position, 1, 0)
        shift_rows = shift_table[clip_index][None].astype(jnp.float32)
        scale_rows = scale_table[clip_index][None].astype(jnp.float32)
        return project(latent, shift_rows, scale_rows, angles, embed_weight, embed_bias, query_weight, key_weight, query_gain, key_gain)
    queries, key_rows = lax.map(one_block, jnp.arange(block_total, dtype=jnp.int32))
    width_all = queries.shape[-1]
    targets = owners * OWN_SLOTS + slots
    query_out = jnp.zeros((RANKS * OWN_SLOTS, block_tokens, width_all), jnp.bfloat16).at[targets].set(queries.reshape(block_total, block_tokens, width_all))
    key_out = jnp.zeros((RANKS * OWN_SLOTS, block_tokens, width_all), jnp.bfloat16).at[targets].set(key_rows.reshape(block_total, block_tokens, width_all))
    return (query_out.reshape(-1, width_all), key_out.reshape(-1, width_all))
```

```python
import functools
import jax
import jax.numpy as jnp
import numpy as np
from jax import lax
from jax.experimental import pallas as pl
from jax.experimental.pallas import tpu as pltpu
from jax.sharding import PartitionSpec as P

F32, BF16, I32 = jnp.float32, jnp.bfloat16, jnp.int32
HIGH = lax.Precision.HIGHEST


def rope_table():
    table = np.zeros((128, 256), np.float32)
    row = lane = 0
    for places, width in ((32, 16), (48, 56), (48, 56)):
        rate = 1.0 / 10000.0 ** (np.arange(0, width, 2, dtype=np.float32) / np.float32(width))
        angle = np.arange(places, dtype=np.float32)[:, None] * rate[None, :].astype(np.float32)
        span = slice(lane, lane + width)
        table[row : row + places, span] = np.repeat(np.cos(angle), 2, axis=1)
        sines = np.repeat(np.sin(angle), 2, axis=1)
        sines[:, 0::2] *= -1.0
        table[row : row + places, 128 + lane : 128 + lane + width] = sines
        row, lane = row + places, lane + width
    return table


def lane_swapped(x):
    width = x.shape[-1]
    even = lax.broadcasted_iota(I32, x.shape, 1) % 2 == 0
    return jnp.where(even, pltpu.roll(x, width - 1, 1), pltpu.roll(x, 1, 1))


def halves(x):
    top = x.astype(BF16)
    return top, (x - top.astype(F32)).astype(BF16)


def finish_kernel(
    info, extents, xt, we, be, shift, scale, gq, gk, table, wq, wk,
    oq, ok,
    w, left, shift_f, scale_f, zz, cs, eps, out, w_sem, o_sem,
):
    slots, channels, tokens = xt.shape
    depth = we.shape[1]
    chunks, _, wide = w.shape
    per = chunks // 2

    def weight_copy(n):
        source = (wq if n < per else wk).at[:, pl.ds((n % per) * wide, wide)]
        return pltpu.make_async_copy(source, w.at[n], w_sem.at[n])

    for n in range(chunks):
        weight_copy(n).start()

    shift_f[...] = shift[...].astype(F32)
    scale_f[...] = scale[...].astype(F32)
    a = we[...].astype(F32)
    a = a - jnp.mean(a, axis=1, keepdims=True)
    b = be[...]
    b = b - jnp.mean(b, axis=1, keepdims=True)
    sub8 = lax.broadcasted_iota(I32, (8, depth), 0)
    b8 = jnp.where(sub8 == 0, b, 0.0)
    whole = jnp.concatenate([a, b8], axis=0)
    gram = lax.dot_general(
        whole, whole, (((1,), (1,)), ((), ())), precision=HIGH, preferred_element_type=F32
    ) * (1.0 / depth)

    extra = []
    for s in range(slots):
        clip = info[s, 0]
        gain = 1.0 + scale_f[pl.ds(clip, 1), :]
        left[pl.ds(s * channels, channels), :] = (a * gain).astype(BF16)
        move = shift_f[pl.ds(clip, 1), :]
        extra.append(jnp.where(sub8 == 0, b * gain, jnp.where(sub8 <= 2, move, 0.0)))
    left[pl.ds(slots * channels, 8 * slots), :] = jnp.concatenate(extra, axis=0).astype(BF16)

    lane = lax.broadcasted_iota(I32, (1, 128), 1)
    sub = lax.broadcasted_iota(I32, (8, tokens), 0)
    both = []
    for g in (gq, gk):
        gain = jnp.concatenate([g[...], lane_swapped(g[...])], axis=1)
        both.extend(halves(table[...] * gain))
    q_table = jnp.concatenate([both[0], both[1]], axis=0)
    k_table = jnp.concatenate([both[2], both[3]], axis=0)
    for s in range(slots):
        x = xt[s].astype(F32)
        x1 = jnp.concatenate([x, jnp.where(sub == 0, 1.0, 0.0)], axis=0)
        y = jnp.dot(gram, x1, precision=HIGH, preferred_element_type=F32)
        var = jnp.maximum(jnp.sum(y * x1, axis=0, keepdims=True), 0.0) + 1e-06
        dev = jnp.sqrt(var)
        dev_hi = dev.astype(BF16).astype(F32)
        more = jnp.where(
            sub == 0, 1.0,
            jnp.where(sub == 1, dev_hi,
                      jnp.where(sub == 2, dev - dev_hi, jnp.where(sub == 3, var * 1e-06, 0.0))),
        )
        zt = jnp.concatenate([x, more, jnp.zeros((128 - channels - 8, tokens), F32)], axis=0)
        z = zt.T
        zb = z.astype(BF16)
        zz[pl.ds(s * tokens, tokens), :] = jnp.concatenate([zb, zb], axis=1)
        eps[s] = jnp.broadcast_to(z[:, channels + 3 : channels + 4], (tokens, 128))
        clip = info[s, 0]
        high = jnp.full((1, 128), extents[clip, 0], I32).astype(F32)
        width = jnp.full((1, 128), extents[clip, 1], I32).astype(F32)
        index = (info[s, 1] + lax.broadcasted_iota(I32, (tokens, 128), 0)).astype(F32)
        frame = jnp.floor((index + 0.5) * (1.0 / (high * width)))
        line = jnp.floor((index + 0.5) * (1.0 / width))
        place = jnp.where(
            lane < 32, frame, jnp.where(lane < 80, line - high * frame + 32.0, index - width * line + 80.0)
        )
        hot = jnp.where(place == lane.astype(F32), 1.0, 0.0).astype(BF16)
        hot = jnp.concatenate([hot, hot], axis=1)
        cs[0, s] = jnp.dot(hot, q_table, preferred_element_type=F32)
        cs[1, s] = jnp.dot(hot, k_table, preferred_element_type=F32)

    r_i = lax.broadcasted_iota(I32, (wide, wide), 0) // 128
    c_i = lax.broadcasted_iota(I32, (wide, wide), 1) // 128
    ones = jnp.where(r_i == c_i, 1.0, 0.0).astype(BF16)
    empty = jnp.zeros((128 - channels - 8, wide), F32)

    def out_copies(n):
        return (
            pltpu.make_async_copy(out.at[n], oq.at[:, pl.ds((n % per) * wide, wide)], o_sem.at[n]),
            pltpu.make_async_copy(out.at[n], ok.at[:, pl.ds((n % per) * wide, wide)], o_sem.at[n]),
        )

    def stack(m, s):
        own = jnp.concatenate(
            [m[s * channels : (s + 1) * channels],
             m[slots * channels + 8 * s : slots * channels + 8 * s + 8], empty], axis=0)
        hi, lo = halves(own)
        return jnp.concatenate([hi, lo], axis=0)

    def chunk(n, carry):
        which = n // per
        pltpu.make_async_copy(wq.at[:, pl.ds(0, wide)], w.at[n], w_sem.at[n]).wait()
        m = jnp.dot(left[...], w[n], preferred_element_type=F32)
        turned = lane_swapped(m)
        for s in range(slots):
            z = zz[pl.ds(s * tokens, tokens), :]
            v = jnp.dot(z, stack(m, s), preferred_element_type=F32)
            vs = jnp.dot(z, stack(turned, s), preferred_element_type=F32)
            power = jnp.dot((v * v).astype(BF16), ones, preferred_element_type=F32)
            c = cs[which, s, :, 0:128]
            sn = cs[which, s, :, 128:256]
            e = eps[s]
            for h in range(wide // 128):
                at = slice(h * 128, (h + 1) * 128)
                inverse = lax.rsqrt(power[:, at] * (1.0 / 128.0) + e)
                o = (v[:, at] * c + vs[:, at] * sn) * inverse
                o = jnp.where(info[s, 2] > 0, o, 0.0)
                out[n, pl.ds(s * tokens, tokens), at] = o.astype(BF16)
        to_q, to_k = out_copies(n)

        @pl.when(n < per)
        def _():
            to_q.start()

        @pl.when(n >= per)
        def _():
            to_k.start()

        return carry

    lax.fori_loop(0, chunks, chunk, 0)
    for n in range(chunks):
        out_copies(n)[n // per].wait()


def finished(info, extents, xt, we, be, shift, scale, gq, gk, wq, wk):
    slots, channels, tokens = xt.shape
    clips, depth = shift.shape
    columns = wq.shape[1]
    wide = 256
    chunks = 2 * columns // wide
    rows = slots * tokens
    vmem = pl.BlockSpec(memory_space=pltpu.VMEM)
    smem = pl.BlockSpec(memory_space=pltpu.SMEM)
    hbm = pl.BlockSpec(memory_space=pl.ANY)
    return pl.pallas_call(
        finish_kernel,
        out_shape=[jax.ShapeDtypeStruct((rows, columns), BF16)] * 2,
        in_specs=[smem, smem] + [vmem] * 8 + [hbm, hbm],
        out_specs=[hbm, hbm],
        scratch_shapes=[
            pltpu.VMEM((chunks, depth, wide), BF16),
            pltpu.VMEM((slots * (channels + 8), depth), BF16),
            pltpu.VMEM((clips, depth), F32),
            pltpu.VMEM((clips, depth), F32),
            pltpu.VMEM((rows, 256), BF16),
            pltpu.VMEM((2, slots, tokens, 256), F32),
            pltpu.VMEM((slots, tokens, 128), F32),
            pltpu.VMEM((chunks, rows, wide), BF16),
            pltpu.SemaphoreType.DMA((chunks,)),
            pltpu.SemaphoreType.DMA((chunks,)),
        ],
        compiler_params=pltpu.CompilerParams(vmem_limit_bytes=60 << 20),
        name="finish",
    )(info, extents, xt, we, be.reshape(1, -1), shift, scale, gq.reshape(1, -1), gk.reshape(1, -1),
      jnp.asarray(rope_table()), wq, wk)


def copy_for_each(x, axis):
    length = lax.axis_size(axis)
    return lax.all_to_all(jnp.broadcast_to(x[None], (length, *x.shape)), axis, 0, 0, tiled=True)


def collected_together(x, axis):
    leaves = jax.tree.leaves(x)
    sequence = sorted(range(len(leaves)), key=lambda k: -leaves[k].size)
    width = (1, *leaves[sequence[0]].shape)[-1]
    lines = [
        jnp.pad(leaves[k].reshape(-1), (0, -leaves[k].size % width)).reshape(-1, width)
        for k in sequence
    ]
    both, at, found = (copy_for_each(jnp.concatenate(lines), axis), 0, {})
    for k, line in zip(sequence, lines):
        share = both[:, at : at + len(line)].reshape(len(both), -1)
        found[k] = share[:, : leaves[k].size].reshape(-1, *leaves[k].shape)
        at += len(line)
    numbers = iter(range(len(leaves)))
    return jax.tree.map(lambda _: found[next(numbers)], x)


def combined_pairwise(pieces, combine):
    while len(jax.tree.leaves(pieces)[0]) > 1:
        pieces = jax.vmap(combine)(
            *(jax.tree.map(lambda part: part[side::2], pieces) for side in (0, 1))
        )
    return jax.tree.map(lambda part: part[0], pieces)


def entering(x, axis, combine, identity):
    length, mine = (lax.axis_size(axis), lax.axis_index(axis))
    passed = jnp.arange(length) < mine

    def kept(part, zero, own):
        part = jnp.where(
            passed.reshape(-1, *(1 for _ in own.shape)), part, jnp.asarray(zero, own.dtype)
        )
        return part

    pieces = collected_together(x, axis)
    return combined_pairwise(jax.tree.map(kept, pieces, identity, x), combine)


def shortened(x):
    return jax.tree.map(lambda a: a.astype(jnp.bfloat16) if a.dtype == jnp.float32 else a, x)


def join_runs(earlier, later):
    first_count, first_clip, first_trail = earlier
    next_count, next_clip, next_trail = later
    joined = (next_trail == next_count) & (first_clip == next_clip)
    trailing = next_trail + jnp.where(joined, first_trail, 0)
    present = next_count > 0
    return (
        first_count + next_count,
        jnp.where(present, next_clip, first_clip),
        jnp.where(present, trailing, first_trail),
    )


def per_device(
    latents,
    clip_ids,
    owners,
    slots,
    extents,
    embed_weight,
    embed_bias,
    shift_table,
    scale_table,
    query_weight,
    key_weight,
    query_gain,
    key_gain,
):
    local_blocks, block_tokens, channels = latents.shape
    ranks = lax.axis_size("seq")
    own_slots = 2 * local_blocks
    block_order = lax.iota(jnp.int32, local_blocks)
    same_before = jnp.sum(
        (
            (clip_ids[None, :] == clip_ids[:, None]) & (block_order[None, :] < block_order[:, None])
        ).astype(jnp.int32),
        axis=1,
    )
    final_clip = clip_ids[local_blocks - 1 :]
    trail_here = jnp.sum((clip_ids == final_clip[0]).astype(jnp.int32)).reshape(1)
    blocks_here = jnp.full((1,), local_blocks, jnp.int32)
    empty = (jnp.zeros((1,), jnp.int32), jnp.full((1,), -1, jnp.int32), jnp.zeros((1,), jnp.int32))
    prior_count, prior_clip, prior_trail = entering(
        (blocks_here, final_clip, trail_here), "seq", join_runs, empty
    )
    offsets = (same_before + jnp.where(clip_ids == prior_clip[0], prior_trail[0], 0)) * block_tokens
    quarter = channels // lax.axis_size("head")
    portion = lax.dynamic_slice_in_dim(
        jnp.transpose(latents, (0, 2, 1)), lax.axis_index("head") * quarter, quarter, 1
    )
    flat_rows = portion.reshape(local_blocks, -1)
    block_info = jnp.stack([owners, slots, clip_ids, offsets, jnp.ones_like(owners)], axis=1)
    slot_order = lax.iota(jnp.int32, own_slots)
    target = owners[:, None] == lax.iota(jnp.int32, ranks)[None, :]
    send_rows = jnp.dot(
        target.T.astype(jnp.bfloat16), flat_rows, preferred_element_type=jnp.float32
    ).astype(jnp.bfloat16)
    send_info = jnp.sum(target.astype(jnp.int32)[:, :, None] * block_info[:, None, :], axis=0)
    got_rows, got_info = (
        lax.all_to_all(send_rows, "seq", split_axis=0, concat_axis=0, tiled=True),
        lax.all_to_all(shortened(send_info), "seq", split_axis=0, concat_axis=0, tiled=True).astype(
            send_info.dtype
        ),
    )
    chosen = (got_info[:, 4][None, :] == 1) & (got_info[:, 1][None, :] == slot_order[:, None])
    slot_rows = jnp.dot(chosen.astype(jnp.bfloat16), got_rows, preferred_element_type=jnp.float32)
    slot_info = jnp.sum(chosen.astype(jnp.int32)[:, :, None] * got_info[None, :, 2:], axis=1)
    slot_latent = slot_rows.astype(jnp.bfloat16).reshape(own_slots, quarter, block_tokens)
    slot_latent = lax.all_gather(slot_latent, "head", axis=1, tiled=True)
    slot_clip = slot_info[:, 0]
    slot_offset = slot_info[:, 1]
    slot_used = slot_info[:, 2]
    info = jnp.stack([slot_clip, slot_offset, slot_used], axis=1)
    return tuple(
        finished(
            info, extents, slot_latent, embed_weight, embed_bias, shift_table, scale_table,
            query_gain, key_gain, query_weight, key_weight,
        )
    )


def solution(mesh):
    placed = (
        P("seq", None, None),
        P("seq"),
        P("seq"),
        P("seq"),
        P(),
        P(),
        P(),
        P(),
        P(),
        P(None, "head"),
        P(None, "head"),
        P(),
        P(),
    )
    return jax.shard_map(
        per_device,
        mesh=mesh,
        in_specs=placed,
        out_specs=(P("seq", "head"), P("seq", "head")),
        check_vma=False,
    )
```

```python
import functools
import jax
import jax.numpy as jnp
import numpy as np
from jax import lax
from jax.experimental import pallas as pl
from jax.experimental.pallas import tpu as pltpu
from jax.sharding import PartitionSpec as P

F32, BF16, I32 = jnp.float32, jnp.bfloat16, jnp.int32
HIGH = lax.Precision.HIGHEST
MESH = pl.DeviceIdType.MESH


def rope_table():
    table = np.zeros((128, 256), np.float32)
    row = lane = 0
    for places, width in ((32, 16), (48, 56), (48, 56)):
        rate = 1.0 / 10000.0 ** (np.arange(0, width, 2, dtype=np.float32) / np.float32(width))
        angle = np.arange(places, dtype=np.float32)[:, None] * rate[None, :].astype(np.float32)
        span = slice(lane, lane + width)
        table[row : row + places, span] = np.repeat(np.cos(angle), 2, axis=1)
        sines = np.repeat(np.sin(angle), 2, axis=1)
        sines[:, 0::2] *= -1.0
        table[row : row + places, 128 + lane : 128 + lane + width] = sines
        row, lane = row + places, lane + width
    return table


def lane_swapped(x):
    width = x.shape[-1]
    even = lax.broadcasted_iota(I32, x.shape, 1) % 2 == 0
    return jnp.where(even, pltpu.roll(x, width - 1, 1), pltpu.roll(x, 1, 1))


def halves(x):
    top = x.astype(BF16)
    return top, (x - top.astype(F32)).astype(BF16)


def finish_kernel(
    meta, extents, xt, we, be, shift, scale, gq, gk, table, wq, wk,
    oq, ok,
    w, left, shift_f, scale_f, zz, cs, eps, out, w_sem, o_sem,
):
    heads, slots, share, tokens = xt.shape
    channels, depth = we.shape
    chunks, _, wide = w.shape
    per = chunks // 2

    def weight_copy(n):
        source = (wq if n < per else wk).at[:, pl.ds((n % per) * wide, wide)]
        return pltpu.make_async_copy(source, w.at[n], w_sem.at[n])

    for n in range(chunks):
        weight_copy(n).start()

    me = lax.axis_index("seq")
    at_lane = lax.broadcasted_iota(I32, (8, 128), 1)
    code = me * slots + lax.broadcasted_iota(I32, (8, 128), 0)
    clip_row = jnp.broadcast_to(meta[0:1, :], (8, 128))
    found = jnp.broadcast_to(meta[1:2, :], (8, 128)) == code
    clip_at = jnp.sum(jnp.where(found, clip_row, 0), axis=1, keepdims=True)
    block_at = jnp.sum(jnp.where(found, at_lane, 0), axis=1, keepdims=True)
    used_at = jnp.sum(jnp.where(found, 1, 0), axis=1, keepdims=True)
    earlier = jnp.sum(jnp.where(clip_row < clip_at, 1, 0), axis=1, keepdims=True)
    offset_at = (block_at - earlier) * tokens
    clip_of = [clip_at[s, 0] for s in range(slots)]
    used_of = [used_at[s, 0] for s in range(slots)]
    offset_of = [offset_at[s, 0] for s in range(slots)]

    shift_f[...] = shift[...].astype(F32)
    scale_f[...] = scale[...].astype(F32)
    a = we[...].astype(F32)
    a = a - jnp.mean(a, axis=1, keepdims=True)
    b = be[...]
    b = b - jnp.mean(b, axis=1, keepdims=True)
    sub8 = lax.broadcasted_iota(I32, (8, depth), 0)
    b8 = jnp.where(sub8 == 0, b, 0.0)
    whole = jnp.concatenate([a, b8], axis=0)
    gram = lax.dot_general(
        whole, whole, (((1,), (1,)), ((), ())), precision=HIGH, preferred_element_type=F32
    ) * (1.0 / depth)

    extra = []
    for s in range(slots):
        clip = clip_of[s]
        gain = 1.0 + scale_f[pl.ds(clip, 1), :]
        left[pl.ds(s * channels, channels), :] = (a * gain).astype(BF16)
        move = shift_f[pl.ds(clip, 1), :]
        extra.append(jnp.where(sub8 == 0, b * gain, jnp.where(sub8 <= 2, move, 0.0)))
    left[pl.ds(slots * channels, 8 * slots), :] = jnp.concatenate(extra, axis=0).astype(BF16)

    lane = lax.broadcasted_iota(I32, (1, 128), 1)
    sub = lax.broadcasted_iota(I32, (8, tokens), 0)
    both = []
    for g in (gq, gk):
        gain = jnp.concatenate([g[...], lane_swapped(g[...])], axis=1)
        both.extend(halves(table[...] * gain))
    q_table = jnp.concatenate([both[0], both[1]], axis=0)
    k_table = jnp.concatenate([both[2], both[3]], axis=0)
    for s in range(slots):
        x = jnp.concatenate([xt[h, s] for h in range(heads)], axis=0).astype(F32)
        x1 = jnp.concatenate([x, jnp.where(sub == 0, 1.0, 0.0)], axis=0)
        y = jnp.dot(gram, x1, precision=HIGH, preferred_element_type=F32)
        var = jnp.maximum(jnp.sum(y * x1, axis=0, keepdims=True), 0.0) + 1e-06
        dev = jnp.sqrt(var)
        dev_hi = dev.astype(BF16).astype(F32)
        more = jnp.where(
            sub == 0, 1.0,
            jnp.where(sub == 1, dev_hi,
                      jnp.where(sub == 2, dev - dev_hi, jnp.where(sub == 3, var * 1e-06, 0.0))),
        )
        zt = jnp.concatenate([x, more, jnp.zeros((128 - channels - 8, tokens), F32)], axis=0)
        z = zt.T
        zb = z.astype(BF16)
        zz[pl.ds(s * tokens, tokens), :] = jnp.concatenate([zb, zb], axis=1)
        eps[s] = jnp.broadcast_to(z[:, channels + 3 : channels + 4], (tokens, 128))
        clip = clip_of[s]
        high = jnp.full((1, 128), extents[0, clip], I32).astype(F32)
        width = jnp.full((1, 128), extents[1, clip], I32).astype(F32)
        index = (offset_of[s] + lax.broadcasted_iota(I32, (tokens, 128), 0)).astype(F32)
        frame = jnp.floor((index + 0.5) * (1.0 / (high * width)))
        line = jnp.floor((index + 0.5) * (1.0 / width))
        place = jnp.where(
            lane < 32, frame, jnp.where(lane < 80, line - high * frame + 32.0, index - width * line + 80.0)
        )
        hot = jnp.where(place == lane.astype(F32), 1.0, 0.0).astype(BF16)
        hot = jnp.concatenate([hot, hot], axis=1)
        cs[0, s] = jnp.dot(hot, q_table, preferred_element_type=F32)
        cs[1, s] = jnp.dot(hot, k_table, preferred_element_type=F32)

    r_i = lax.broadcasted_iota(I32, (wide, wide), 0) // 128
    c_i = lax.broadcasted_iota(I32, (wide, wide), 1) // 128
    ones = jnp.where(r_i == c_i, 1.0, 0.0).astype(BF16)
    empty = jnp.zeros((128 - channels - 8, wide), F32)

    def out_copies(n):
        return (
            pltpu.make_async_copy(out.at[n], oq.at[:, pl.ds((n % per) * wide, wide)], o_sem.at[n]),
            pltpu.make_async_copy(out.at[n], ok.at[:, pl.ds((n % per) * wide, wide)], o_sem.at[n]),
        )

    def stack(m, s):
        own = jnp.concatenate(
            [m[s * channels : (s + 1) * channels],
             m[slots * channels + 8 * s : slots * channels + 8 * s + 8], empty], axis=0)
        hi, lo = halves(own)
        return jnp.concatenate([hi, lo], axis=0)

    def chunk(n, carry):
        which = n // per
        pltpu.make_async_copy(wq.at[:, pl.ds(0, wide)], w.at[n], w_sem.at[n]).wait()
        m = jnp.dot(left[...], w[n], preferred_element_type=F32)
        turned = lane_swapped(m)
        for s in range(slots):
            z = zz[pl.ds(s * tokens, tokens), :]
            v = jnp.dot(z, stack(m, s), preferred_element_type=F32)
            vs = jnp.dot(z, stack(turned, s), preferred_element_type=F32)
            power = jnp.dot((v * v).astype(BF16), ones, preferred_element_type=F32)
            c = cs[which, s, :, 0:128]
            sn = cs[which, s, :, 128:256]
            e = eps[s]
            for h in range(wide // 128):
                at = slice(h * 128, (h + 1) * 128)
                inverse = lax.rsqrt(power[:, at] * (1.0 / 128.0) + e)
                o = (v[:, at] * c + vs[:, at] * sn) * inverse
                o = jnp.where(used_of[s] > 0, o, 0.0)
                out[n, pl.ds(s * tokens, tokens), at] = o.astype(BF16)
        to_q, to_k = out_copies(n)

        @pl.when(n < per)
        def _():
            to_q.start()

        @pl.when(n >= per)
        def _():
            to_k.start()

        return carry

    lax.fori_loop(0, chunks, chunk, 0)
    for n in range(chunks):
        out_copies(n)[n // per].wait()


def finished(meta, extents, xt, we, be, shift, scale, gq, gk, wq, wk):
    heads, slots, share, tokens = xt.shape
    channels = heads * share
    clips, depth = shift.shape
    columns = wq.shape[1]
    wide = 256
    chunks = 2 * columns // wide
    rows = slots * tokens
    vmem = pl.BlockSpec(memory_space=pltpu.VMEM)
    smem = pl.BlockSpec(memory_space=pltpu.SMEM)
    hbm = pl.BlockSpec(memory_space=pl.ANY)
    return pl.pallas_call(
        finish_kernel,
        out_shape=[jax.ShapeDtypeStruct((rows, columns), BF16)] * 2,
        in_specs=[vmem, smem] + [vmem] * 8 + [hbm, hbm],
        out_specs=[hbm, hbm],
        scratch_shapes=[
            pltpu.VMEM((chunks, depth, wide), BF16),
            pltpu.VMEM((slots * (channels + 8), depth), BF16),
            pltpu.VMEM((clips, depth), F32),
            pltpu.VMEM((clips, depth), F32),
            pltpu.VMEM((rows, 256), BF16),
            pltpu.VMEM((2, slots, tokens, 256), F32),
            pltpu.VMEM((slots, tokens, 128), F32),
            pltpu.VMEM((chunks, rows, wide), BF16),
            pltpu.SemaphoreType.DMA((chunks,)),
            pltpu.SemaphoreType.DMA((chunks,)),
        ],
        compiler_params=pltpu.CompilerParams(vmem_limit_bytes=60 << 20),
        name="finish",
    )(meta, extents.T, xt, we, be.reshape(1, -1), shift, scale, gq.reshape(1, -1), gk.reshape(1, -1),
      jnp.asarray(rope_table()), wq, wk)


def routing_kernel(
    clips, owners, slot_ids, latents,
    xt, meta,
    near, tags, frame, wanted, side, side_tags,
    in_sem, s1, r1, t1, u1, s2, r2, t2, u2, s3, r3,
    *, deep, across,
):
    me = lax.axis_index("seq")
    x = lax.axis_index("head")
    heads = xt.shape[0]
    blocks, share, tokens = near.shape[1:]
    group = 2 * across
    plane, within = me // group, me % group
    y, core = within // 2, within % 2
    own = xt.shape[1]

    def z_peer(r):
        return {"seq": (plane + r) % deep * group + within}

    def y_peer(r):
        return {"seq": plane * group + (y + r // 2) % across * 2 + (core + r) % 2}

    def x_peer(r):
        return {"head": (x + r) % heads}

    z_steps = sorted(range(1, deep), key=lambda r: -min(r, deep - r))
    y_steps = sorted(range(1, group), key=lambda r: -min(r // 2, across - r // 2))
    x_steps = sorted(range(1, heads), key=lambda r: -min(r, heads - r))
    barrier = pltpu.get_barrier_semaphore()
    for peer in [z_peer(r) for r in z_steps] + [y_peer(r) for r in y_steps] + [x_peer(r) for r in x_steps]:
        pl.semaphore_signal(barrier, inc=1, device_id=peer, device_id_type=MESH)
    take = pltpu.make_async_copy(latents.at[:, pl.ds(x * share, share), :], near.at[0], in_sem)
    take.start()

    sub = lax.broadcasted_iota(I32, (8, 128), 0)
    lane = lax.broadcasted_iota(I32, (8, 128), 1)
    tag = jnp.zeros((8, 128), I32)
    for j in range(blocks):
        code = owners[j] * own + slot_ids[j]
        here = lane == blocks * me + j
        tag = tag + jnp.where(here & (sub == 0), clips[j], 0)
        tag = tag + jnp.where(here & (sub == 1), code, 0)
        tag = tag + jnp.where(sub == 2 + j, code, 0)
    tags[0] = tag
    for r in range(group):
        for s in range(own):
            code = y_peer(r)["seq"] * own + s
            wanted[r * own + s] = jnp.full((share, tokens), code, I32).astype(F32).astype(BF16)
    take.wait()
    pl.semaphore_wait(barrier, deep + group + heads - 3)

    def z_copies(r):
        return (
            pltpu.make_async_remote_copy(
                near.at[0], near.at[r], s1.at[r], r1.at[r], device_id=z_peer(r), device_id_type=MESH),
            pltpu.make_async_remote_copy(
                tags.at[0], tags.at[r], t1.at[r], u1.at[r], device_id=z_peer(r), device_id_type=MESH),
        )

    sent = []
    for r in z_steps:
        data, words = z_copies(r)
        data.start()
        words.start()
        sent += [data, words]

    def sort_in(r, first):
        for j in range(blocks):
            code = jnp.broadcast_to(tags[r, 2 + j : 3 + j, :], (share, 128)).astype(F32).astype(BF16)
            code = jnp.concatenate([code] * (tokens // 128), axis=1)
            hit = wanted[...] == code[None]
            before = jnp.zeros(frame.shape, BF16) if first and j == 0 else frame[...]
            frame[...] = jnp.where(hit, near[r, j][None], before)

    sort_in(0, True)
    total = tags[0]
    for r in reversed(z_steps):
        data, words = z_copies(r)
        data.wait_recv()
        words.wait_recv()
        sort_in(r, False)
        total = total + tags[r]
    side_tags[0] = total

    def y_copies(r):
        return (
            pltpu.make_async_remote_copy(
                frame.at[pl.ds(r * own, own)], side.at[r], s2.at[r], r2.at[r],
                device_id=y_peer(r), device_id_type=MESH),
            pltpu.make_async_remote_copy(
                side_tags.at[0], side_tags.at[r], t2.at[r], u2.at[r],
                device_id=y_peer(r), device_id_type=MESH),
        )

    for r in y_steps:
        data, words = y_copies(r)
        data.start()
        words.start()
        sent += [data, words]
    mine = frame[0:own]
    for r in reversed(y_steps):
        data, words = y_copies(r)
        data.wait_recv()
        words.wait_recv()
        mine = mine + side[r]
        total = total + side_tags[r]
    xt[x] = mine

    def x_copy(r):
        return pltpu.make_async_remote_copy(
            xt.at[x], xt.at[x], s3.at[r], r3.at[r], device_id=x_peer(r), device_id_type=MESH)

    for r in x_steps:
        copy = x_copy(r)
        copy.start()
        sent.append(copy)
    meta[...] = total
    for r in reversed(x_steps):
        at = xt.at[(x + heads - r) % heads]
        pltpu.make_async_remote_copy(
            at, at, s3.at[r], r3.at[r], device_id=x_peer(r), device_id_type=MESH).wait_recv()
    for copy in sent:
        copy.wait_send()


def routed(clips, owners, slot_ids, latents, own, heads, deep, across):
    blocks, channels, tokens = latents.shape
    share = channels // heads
    group = 2 * across
    vmem = pl.BlockSpec(memory_space=pltpu.VMEM)
    smem = pl.BlockSpec(memory_space=pltpu.SMEM)
    hbm = pl.BlockSpec(memory_space=pl.ANY)
    dma = pltpu.SemaphoreType.DMA
    return pl.pallas_call(
        functools.partial(routing_kernel, deep=deep, across=across),
        out_shape=[
            jax.ShapeDtypeStruct((heads, own, share, tokens), BF16),
            jax.ShapeDtypeStruct((8, 128), I32),
        ],
        in_specs=[smem, smem, smem, hbm],
        out_specs=[vmem, vmem],
        scratch_shapes=[
            pltpu.VMEM((deep, blocks, share, tokens), BF16),
            pltpu.VMEM((deep, 8, 128), I32),
            pltpu.VMEM((group * own, share, tokens), BF16),
            pltpu.VMEM((group * own, share, tokens), BF16),
            pltpu.VMEM((group, own, share, tokens), BF16),
            pltpu.VMEM((group, 8, 128), I32),
            dma,
            dma((deep,)), dma((deep,)), dma((deep,)), dma((deep,)),
            dma((group,)), dma((group,)), dma((group,)), dma((group,)),
            dma((heads,)), dma((heads,)),
        ],
        compiler_params=pltpu.CompilerParams(
            collective_id=0, has_side_effects=True, vmem_limit_bytes=16 << 20),
        name="routing",
    )(clips, owners, slot_ids, latents)


def per_device(
    across, latents, clip_ids, owners, slots, extents, embed_weight, embed_bias, shift_table, scale_table,
    query_weight, key_weight, query_gain, key_gain,
):
    local = latents.shape[0]
    own = 2 * local
    heads, ranks = lax.axis_size("head"), lax.axis_size("seq")
    xt, meta = routed(
        clip_ids, owners, slots, jnp.transpose(latents, (0, 2, 1)), own, heads, ranks // (2 * across), across
    )
    return tuple(
        finished(
            meta, extents, xt, embed_weight, embed_bias, shift_table, scale_table,
            query_gain, key_gain, query_weight, key_weight,
        )
    )


def solution(mesh):
    placed = (
        P("seq", None, None),
        P("seq"),
        P("seq"),
        P("seq"),
        P(),
        P(),
        P(),
        P(),
        P(),
        P(None, "head"),
        P(None, "head"),
        P(),
        P(),
    )
    return jax.shard_map(
        functools.partial(per_device, 4),
        mesh=mesh,
        in_specs=placed,
        out_specs=(P("seq", "head"), P("seq", "head")),
        check_vma=False,
    )
```

```python
import functools
import jax
import jax.numpy as jnp
import numpy as np
from jax import lax
from jax.experimental import pallas as pl
from jax.experimental.pallas import tpu as pltpu
from jax.sharding import PartitionSpec as P

F32, BF16, I32 = jnp.float32, jnp.bfloat16, jnp.int32
HIGH = lax.Precision.HIGHEST
MESH = pl.DeviceIdType.MESH
WIDE = 256
HBM = pl.BlockSpec(memory_space=pltpu.HBM)
VMEM = pl.BlockSpec(memory_space=pltpu.VMEM)


def rope_table():
    table = np.zeros((128, 256), np.float32)
    row = lane = 0
    for places, width in ((32, 16), (48, 56), (48, 56)):
        rate = 1.0 / 10000.0 ** (np.arange(0, width, 2, dtype=np.float32) / np.float32(width))
        angle = np.arange(places, dtype=np.float32)[:, None] * rate[None, :].astype(np.float32)
        span = slice(lane, lane + width)
        table[row : row + places, span] = np.repeat(np.cos(angle), 2, axis=1)
        sines = np.repeat(np.sin(angle), 2, axis=1)
        sines[:, 0::2] *= -1.0
        table[row : row + places, 128 + lane : 128 + lane + width] = sines
        row, lane = row + places, lane + width
    return table


def lane_swapped(x):
    width = x.shape[-1]
    even = lax.broadcasted_iota(I32, x.shape, 1) % 2 == 0
    return jnp.where(even, pltpu.roll(x, width - 1, 1), pltpu.roll(x, 1, 1))


def halves(x):
    top = x.astype(BF16)
    return top, (x - top.astype(F32)).astype(BF16)


def routing_kernel(
    clips_h, owners_h, slots_h, latents, extents_h, we_h, be_h, shift_h, scale_h, gq_h, gk_h, table_h, wq, wk,
    xt, m_out, cs, gram_out, use,
    clips, owners, slot_ids, extents, we, be, shift, scale, gq, gk, table, w, left, base, halved,
    near, tags, frame, wanted, side, side_tags,
    in_sem, w_sem, s1, r1, t1, u1, s2, r2, t2, u2, s3, r3,
    *, deep, across,
):
    me = lax.axis_index("seq")
    x = lax.axis_index("head")
    heads = xt.shape[0]
    blocks, share, tokens = near.shape[1:]
    group = 2 * across
    plane, within = me // group, me % group
    y, core = within // 2, within % 2
    own = xt.shape[1]
    channels, depth = we_h.shape
    per = w.shape[0] // 2

    def z_peer(r):
        return {"seq": (plane + r) % deep * group + within}

    def y_peer(r):
        return {"seq": plane * group + (y + r // 2) % across * 2 + (core + r) % 2}

    def x_peer(r):
        return {"head": (x + r) % heads}

    z_steps = sorted(range(1, deep), key=lambda r: -min(r, deep - r))
    y_steps = sorted(range(1, group), key=lambda r: -min(r // 2, across - r // 2))
    x_steps = sorted(range(1, heads), key=lambda r: -min(r, heads - r))
    barrier = pltpu.get_barrier_semaphore()
    for peer in [z_peer(r) for r in z_steps] + [y_peer(r) for r in y_steps] + [x_peer(r) for r in x_steps]:
        pl.semaphore_signal(barrier, inc=1, device_id=peer, device_id_type=MESH)

    takes = [
        pltpu.make_async_copy(source, place, in_sem.at[k])
        for k, (source, place) in enumerate((
            (clips_h, clips), (owners_h, owners), (slots_h, slot_ids),
            (latents.at[:, pl.ds(x * share, share), :], near.at[0]),
            (we_h, we), (be_h, be), (gq_h, gq), (gk_h, gk), (table_h, table),
            (shift_h, shift), (scale_h, scale), (extents_h, extents),
        ))
    ]
    weights = [
        pltpu.make_async_copy(source.at[:, pl.ds(n * WIDE, WIDE)], w.at[k * per + n], w_sem.at[k * per + n])
        for n in range(per) for k, source in enumerate((wq, wk))
    ]
    for copy in takes + weights:
        copy.start()

    sub = lax.broadcasted_iota(I32, (8, 128), 0)
    lane = lax.broadcasted_iota(I32, (8, 128), 1)
    for r in range(group):
        for s in range(own):
            code = y_peer(r)["seq"] * own + s
            wanted[r * own + s] = jnp.full((share, tokens), code, I32).astype(F32).astype(BF16)
    for copy in takes[:3]:
        copy.wait()
    tag = jnp.zeros((8, 128), I32)
    for j in range(blocks):
        code = owners[j] * own + slot_ids[j]
        here = lane == blocks * me + j
        tag = tag + jnp.where(here & (sub == 0), clips[j], 0)
        tag = tag + jnp.where(here & (sub == 1), code, 0)
        tag = tag + jnp.where(sub == 2 + j, code, 0)
    tags[0] = tag
    takes[3].wait()
    pl.semaphore_wait(barrier, deep + group + heads - 3)

    def z_copies(r):
        return (
            pltpu.make_async_remote_copy(
                near.at[0], near.at[r], s1.at[r], r1.at[r], device_id=z_peer(r), device_id_type=MESH),
            pltpu.make_async_remote_copy(
                tags.at[0], tags.at[r], t1.at[r], u1.at[r], device_id=z_peer(r), device_id_type=MESH),
        )

    sent = []
    for r in z_steps:
        data, words = z_copies(r)
        data.start()
        words.start()
        sent += [data, words]

    def sort_in(r, first):
        for j in range(blocks):
            code = jnp.broadcast_to(tags[r, 2 + j : 3 + j, :], (share, 128)).astype(F32).astype(BF16)
            code = jnp.concatenate([code] * (tokens // 128), axis=1)
            hit = wanted[...] == code[None]
            before = jnp.zeros(frame.shape, BF16) if first and j == 0 else frame[...]
            frame[...] = jnp.where(hit, near[r, j][None], before)

    for copy in takes[4:]:
        copy.wait()
    a = we[...].astype(F32)
    a = a - jnp.mean(a, axis=1, keepdims=True)
    b = be[...]
    b = b - jnp.mean(b, axis=1, keepdims=True)
    sub16 = lax.broadcasted_iota(I32, (16, depth), 0)
    base[0:channels, :] = a
    base[channels : channels + 16, :] = jnp.where(sub16 == 0, b, 0.0)
    gram = lax.dot_general(
        base[...], base[...], (((1,), (1,)), ((), ())), precision=HIGH, preferred_element_type=F32
    ) * (1.0 / depth)
    for k in range(3):
        part = gram.astype(BF16)
        gram_out[k] = part
        gram = gram - part.astype(F32)
    for k, g in enumerate((gq, gk)):
        gain = jnp.concatenate([g[...], lane_swapped(g[...])], axis=1)
        hi, lo = halves(table[...] * gain)
        halved[k, 0:128, :] = hi
        halved[k, 128:256, :] = lo

    sort_in(0, True)
    total = tags[0]
    for r in reversed(z_steps):
        data, words = z_copies(r)
        data.wait_recv()
        words.wait_recv()
        sort_in(r, False)
        total = total + tags[r]
    side_tags[0] = total

    def y_copies(r):
        return (
            pltpu.make_async_remote_copy(
                frame.at[pl.ds(r * own, own)], side.at[r], s2.at[r], r2.at[r],
                device_id=y_peer(r), device_id_type=MESH),
            pltpu.make_async_remote_copy(
                side_tags.at[0], side_tags.at[r], t2.at[r], u2.at[r],
                device_id=y_peer(r), device_id_type=MESH),
        )

    for r in y_steps:
        data, words = y_copies(r)
        words.start()
        data.start()
        sent += [data, words]
    mine = frame[0:own]
    for r in reversed(y_steps):
        data, words = y_copies(r)
        data.wait_recv()
        words.wait_recv()
        mine = mine + side[r]
        total = total + side_tags[r]
    xt[x] = mine

    def x_copy(r):
        return pltpu.make_async_remote_copy(
            xt.at[x], xt.at[x], s3.at[r], r3.at[r], device_id=x_peer(r), device_id_type=MESH)

    for r in x_steps:
        copy = x_copy(r)
        copy.start()
        sent.append(copy)

    clip_row = jnp.broadcast_to(total[0:1, :], (8, 128))
    found = jnp.broadcast_to(total[1:2, :], (8, 128)) == me * own + sub
    clip_at = jnp.sum(jnp.where(found, clip_row, 0), axis=1, keepdims=True)
    block_at = jnp.sum(jnp.where(found, lane, 0), axis=1, keepdims=True)
    used_at = jnp.sum(jnp.where(found, 1, 0), axis=1, keepdims=True)
    earlier = jnp.sum(jnp.where(clip_row < clip_at, 1, 0), axis=1, keepdims=True)
    offset_at = (block_at - earlier) * tokens
    use[...] = jnp.broadcast_to(used_at.astype(F32), (8, 128))
    count = shift.shape[0]
    among = lax.broadcasted_iota(I32, (8, count), 1) == clip_at
    high_at = jnp.sum(jnp.where(among, extents[0:1, :], 0), axis=1, keepdims=True).astype(F32)
    wide_at = jnp.sum(jnp.where(among, extents[1:2, :], 0), axis=1, keepdims=True).astype(F32)
    pick = jnp.where(among, 1.0, 0.0).astype(BF16)
    moves = jnp.dot(pick, shift[...], preferred_element_type=F32)
    gains = 1.0 + jnp.dot(pick, scale[...], preferred_element_type=F32)
    sub8 = lax.broadcasted_iota(I32, (8, depth), 0)
    extra = []
    for s in range(own):
        gain = gains[s : s + 1, :]
        left[s * channels : (s + 1) * channels, :] = (base[0:channels, :] * gain).astype(BF16)
        middle = base[channels : channels + 1, :] * gain
        extra.append(jnp.where(sub8 == 0, middle, jnp.where(sub8 <= 2, moves[s : s + 1, :], 0.0)))
    left[own * channels :, :] = jnp.concatenate(extra, axis=0).astype(BF16)
    for copy in weights:
        copy.wait()

    def project(n, carry):
        m_out[n] = jnp.dot(left[...], w[n], preferred_element_type=F32)
        m_out[n + per] = jnp.dot(left[...], w[n + per], preferred_element_type=F32)
        return carry

    lax.fori_loop(0, per, project, 0)

    lane_f = lax.broadcasted_iota(I32, (1, 128), 1).astype(F32)
    steps = lax.broadcasted_iota(I32, (tokens, 128), 0).astype(F32)
    for s in range(own):
        high, wide = high_at[s : s + 1, :], wide_at[s : s + 1, :]
        high, wide = jnp.maximum(high, 1.0), jnp.maximum(wide, 1.0)
        index = offset_at[s : s + 1, :].astype(F32) + steps
        frames = jnp.floor((index + 0.5) * (1.0 / (high * wide)))
        lines = jnp.floor((index + 0.5) * (1.0 / wide))
        place = jnp.where(
            lane_f < 32.0, frames,
            jnp.where(lane_f < 80.0, lines - high * frames + 32.0, index - wide * lines + 80.0),
        )
        hot = jnp.where(place == lane_f, 1.0, 0.0).astype(BF16)
        hot = jnp.concatenate([hot, hot], axis=1)
        cs[0, s] = jnp.dot(hot, halved[0], preferred_element_type=F32)
        cs[1, s] = jnp.dot(hot, halved[1], preferred_element_type=F32)

    for r in reversed(x_steps):
        at = xt.at[(x + heads - r) % heads]
        pltpu.make_async_remote_copy(
            at, at, s3.at[r], r3.at[r], device_id=x_peer(r), device_id_type=MESH).wait_recv()
    for copy in sent:
        copy.wait_send()


def routed(
    across, clips, owners, slot_ids, latents, extents, we, be, shift, scale, gq, gk, wq, wk
):
    blocks, channels, tokens = latents.shape
    own = 2 * blocks
    heads, deep = lax.axis_size("head"), lax.axis_size("seq") // (2 * across)
    share = channels // heads
    group = 2 * across
    depth, columns = wq.shape
    chunks = 2 * columns // WIDE
    dma, room = pltpu.SemaphoreType.DMA, pltpu.VMEM
    table = jnp.asarray(rope_table())
    flat = [v.reshape(1, -1) for v in (be, gq, gk)]
    rows = own * (channels + 8)
    args = (clips, owners, slot_ids, latents, extents.T, we, flat[0], shift, scale, flat[1], flat[2], table, wq, wk)
    return pl.pallas_call(
        functools.partial(routing_kernel, deep=deep, across=across),
        out_shape=[
            jax.ShapeDtypeStruct((heads, own, share, tokens), BF16),
            jax.ShapeDtypeStruct((chunks, rows, WIDE), F32),
            jax.ShapeDtypeStruct((2, own, tokens, 256), F32),
            jax.ShapeDtypeStruct((3, channels + 16, channels + 16), BF16),
            jax.ShapeDtypeStruct((8, 128), F32),
        ],
        in_specs=[HBM] * len(args),
        out_specs=[VMEM] * 5,
        scratch_shapes=[
            pltpu.SMEM(clips.shape, I32), pltpu.SMEM(clips.shape, I32), pltpu.SMEM(clips.shape, I32),
            *(room(v.shape, v.dtype) for v in (args[4], we, flat[0], shift, scale, flat[1], flat[2], table)),
            room((chunks, depth, WIDE), BF16),
            room((rows, depth), BF16),
            room((channels + 16, depth), F32),
            room((2, 256, 256), BF16),
            room((deep, blocks, share, tokens), BF16),
            room((deep, 8, 128), I32),
            room((group * own, share, tokens), BF16),
            room((group * own, share, tokens), BF16),
            room((group, own, share, tokens), BF16),
            room((group, 8, 128), I32),
            dma((12,)), dma((chunks,)),
            dma((deep,)), dma((deep,)), dma((deep,)), dma((deep,)),
            dma((group,)), dma((group,)), dma((group,)), dma((group,)),
            dma((heads,)), dma((heads,)),
        ],
        compiler_params=pltpu.CompilerParams(
            collective_id=0, has_side_effects=True, vmem_limit_bytes=28 << 20),
        name="routing",
    )(*(pltpu.with_memory_space_constraint(v, pltpu.HBM) for v in args))


def finish_kernel(xt, m_in, cs, gram, use, oq, ok, zz, eps, out, o_sem):
    heads, slots, share, tokens = xt.shape
    channels = heads * share
    chunks, _, wide = m_in.shape
    per = chunks // 2
    sub = lax.broadcasted_iota(I32, (16, tokens), 0)
    for s in range(slots):
        x = jnp.concatenate([xt[h, s] for h in range(heads)], axis=0)
        x1 = jnp.concatenate([x, jnp.where(sub == 0, 1.0, 0.0).astype(BF16)], axis=0)
        y = sum(jnp.dot(gram[k], x1, preferred_element_type=F32) for k in range(3))
        xf = x1.astype(F32)
        var = jnp.maximum(jnp.sum(y * xf, axis=0, keepdims=True), 0.0) + 1e-06
        dev = jnp.sqrt(var)
        dev_hi = dev.astype(BF16).astype(F32)
        more = jnp.where(
            sub == 0, 1.0,
            jnp.where(sub == 1, dev_hi,
                      jnp.where(sub == 2, dev - dev_hi, jnp.where(sub == 3, var * 1e-06, 0.0))),
        )
        zt = jnp.concatenate([xf[0:channels], more, jnp.zeros((112 - channels, tokens), F32)], axis=0)
        z = zt.T
        eps[s] = jnp.broadcast_to(z[:, channels + 3 : channels + 4], (tokens, 128))
        zb = (z * use[s : s + 1, :]).astype(BF16)
        zz[s] = jnp.concatenate([zb, zb], axis=1)

    r_i = lax.broadcasted_iota(I32, (wide, wide), 0) // 128
    c_i = lax.broadcasted_iota(I32, (wide, wide), 1) // 128
    ones = jnp.where(r_i == c_i, 1.0 / 128.0, 0.0).astype(BF16)
    empty = jnp.zeros((128 - channels - 8, wide), F32)

    def stack(m, s):
        own = jnp.concatenate(
            [m[s * channels : (s + 1) * channels],
             m[slots * channels + 8 * s : slots * channels + 8 * s + 8], empty], axis=0)
        hi, lo = halves(own)
        return jnp.concatenate([hi, lo], axis=0)

    def out_copy(n, place):
        return pltpu.make_async_copy(
            out.at[n], place.at[:, pl.ds(n % per * wide, wide)], o_sem.at[n])

    def chunk(n, carry):
        which = n // per
        m = m_in[n]
        turned = lane_swapped(m)
        for s in range(slots):
            z = zz[s]
            v = jnp.dot(z, stack(m, s), preferred_element_type=F32)
            vs = jnp.dot(z, stack(turned, s), preferred_element_type=F32)
            power = jnp.dot((v * v).astype(BF16), ones, preferred_element_type=F32)
            c = cs[which, s, :, 0:128]
            sn = cs[which, s, :, 128:256]
            e = eps[s]
            for h in range(wide // 128):
                at = slice(h * 128, (h + 1) * 128)
                o = (v[:, at] * c + vs[:, at] * sn) * lax.rsqrt(power[:, at] + e)
                out[n, s * tokens : (s + 1) * tokens, at] = o.astype(BF16)

        @pl.when(n < per)
        def _():
            out_copy(n, oq).start()

        @pl.when(n >= per)
        def _():
            out_copy(n, ok).start()

        return carry

    lax.fori_loop(0, chunks, chunk, 0)
    for n in range(chunks):
        out_copy(n, oq if n < per else ok).wait()


def finished(xt, m, cs, gram, use):
    heads, slots, share, tokens = xt.shape
    chunks, _, wide = m.shape
    rows = slots * tokens
    return pl.pallas_call(
        finish_kernel,
        out_shape=[jax.ShapeDtypeStruct((rows, chunks // 2 * wide), BF16)] * 2,
        in_specs=[VMEM] * 5,
        out_specs=[pl.BlockSpec(memory_space=pl.ANY)] * 2,
        scratch_shapes=[
            pltpu.VMEM((slots, tokens, 256), BF16),
            pltpu.VMEM((slots, tokens, 128), F32),
            pltpu.VMEM((chunks, rows, wide), BF16),
            pltpu.SemaphoreType.DMA((chunks,)),
        ],
        compiler_params=pltpu.CompilerParams(vmem_limit_bytes=28 << 20),
        name="finish",
    )(xt, m, cs, gram, use)


def per_device(
    across, latents, clip_ids, owners, slots, extents, embed_weight, embed_bias, shift_table, scale_table,
    query_weight, key_weight, query_gain, key_gain,
):
    parts = routed(
        across, clip_ids, owners, slots, jnp.transpose(latents, (0, 2, 1)), extents, embed_weight, embed_bias,
        shift_table, scale_table, query_gain, key_gain, query_weight, key_weight,
    )
    return tuple(finished(*parts))


def solution(mesh):
    placed = (
        P("seq", None, None),
        P("seq"),
        P("seq"),
        P("seq"),
        P(),
        P(),
        P(),
        P(),
        P(),
        P(None, "head"),
        P(None, "head"),
        P(),
        P(),
    )
    return jax.shard_map(
        functools.partial(per_device, 4),
        mesh=mesh,
        in_specs=placed,
        out_specs=(P("seq", "head"), P("seq", "head")),
        check_vma=False,
    )
```

```python
import functools
import jax
import jax.numpy as jnp
import numpy as np
from jax import lax
from jax.experimental import pallas as pl
from jax.experimental.pallas import tpu as pltpu
from jax.sharding import PartitionSpec as P

F32, BF16, I32 = jnp.float32, jnp.bfloat16, jnp.int32
HIGH = lax.Precision.HIGHEST
MESH = pl.DeviceIdType.MESH
WIDE = 256
HBM = pl.BlockSpec(memory_space=pltpu.HBM)
VMEM = pl.BlockSpec(memory_space=pltpu.VMEM)


def rope_table():
    table = np.zeros((128, 256), np.float32)
    row = lane = 0
    for places, width in ((32, 16), (48, 56), (48, 56)):
        rate = 1.0 / 10000.0 ** (np.arange(0, width, 2, dtype=np.float32) / np.float32(width))
        angle = np.arange(places, dtype=np.float32)[:, None] * rate[None, :].astype(np.float32)
        span = slice(lane, lane + width)
        table[row : row + places, span] = np.repeat(np.cos(angle), 2, axis=1)
        sines = np.repeat(np.sin(angle), 2, axis=1)
        sines[:, 0::2] *= -1.0
        table[row : row + places, 128 + lane : 128 + lane + width] = sines
        row, lane = row + places, lane + width
    return table


def lane_swapped(x):
    width = x.shape[-1]
    even = lax.broadcasted_iota(I32, x.shape, 1) % 2 == 0
    return jnp.where(even, pltpu.roll(x, width - 1, 1), pltpu.roll(x, 1, 1))


def halves(x):
    top = x.astype(BF16)
    return top, (x - top.astype(F32)).astype(BF16)


def routing_kernel(
    clips_h, owners_h, slots_h, latents, extents_h, we_h, be_h, shift_h, scale_h, gq_h, gk_h, table_h, wq, wk,
    xt, m_out, cs, gram_out, use,
    clips, owners, slot_ids, extents, we, be, shift, scale, gq, gk, table, w, left, base, halved,
    mine, near, frame, wanted, side, ready,
    in_sem, w_sem, s1, r1, s2, r2, s3, r3,
    *, deep, across,
):
    me = lax.axis_index("seq")
    x = lax.axis_index("head")
    heads = xt.shape[0] // 2
    blocks, channels, tokens = latents.shape
    share = channels // (2 * heads)
    pair = tokens // 128
    group = 2 * across
    plane, y, core = me // group, me % group // 2, me % 2
    own = 2 * blocks
    both = 2 * own
    depth = we_h.shape[1]
    per = w.shape[0] // 2

    def z_peer(q):
        return {"seq": ((plane + q // 2) % deep * across + y) * 2 + (core + q) % 2}

    def y_peer(r):
        return {"seq": (plane * across + (y + r) % across) * 2 + core}

    def x_peer(q):
        return {"seq": me - core + (core + q) % 2, "head": (x + q // 2) % heads}

    z_steps = sorted(range(1, 2 * deep), key=lambda q: -min(q // 2, deep - q // 2))
    y_steps = sorted(range(1, across), key=lambda r: -min(r, across - r))
    x_steps = sorted(range(1, 2 * heads), key=lambda q: -min(q // 2, heads - q // 2))
    peers = [z_peer(q) for q in z_steps] + [y_peer(r) for r in y_steps] + [x_peer(q) for q in x_steps if q != 1]
    barrier = pltpu.get_barrier_semaphore()
    for peer in peers:
        pl.semaphore_signal(barrier, inc=1, device_id=peer, device_id_type=MESH)

    takes = [
        pltpu.make_async_copy(source, place, in_sem.at[k])
        for k, (source, place) in enumerate((
            (clips_h, clips), (owners_h, owners), (slots_h, slot_ids),
            *((latents.at[:, pl.ds(pl.multiple_of((2 * x + (core + k) % 2) * share, share), share),
                          h * 128 : (h + 1) * 128],
               mine.at[k, h * blocks : (h + 1) * blocks]) for k in range(2) for h in range(pair)),
            (we_h, we), (be_h, be), (gq_h, gq), (gk_h, gk), (table_h, table),
            (shift_h, shift), (scale_h, scale), (extents_h, extents),
        ))
    ]
    weights = [
        pltpu.make_async_copy(source.at[:, pl.ds(n * WIDE, WIDE)], w.at[k * per + n], w_sem.at[k * per + n])
        for n in range(per) for k, source in enumerate((wq, wk))
    ]
    for copy in takes + weights:
        copy.start()
    first = 3 + 2 * pair

    sub = lax.broadcasted_iota(I32, (8, 128), 0)
    lane = lax.broadcasted_iota(I32, (8, 128), 1)
    for r in range(across):
        for s in range(both):
            code = (plane * across + (y + r) % across) * both + s
            wanted[r, s] = jnp.full((share, 128), code, I32).astype(F32).astype(BF16)
    for copy in takes[:3]:
        copy.wait()
    tag = jnp.zeros((8, 128), I32)
    for j in range(blocks):
        code = owners[j] * own + slot_ids[j]
        here = lane == blocks * me + j
        tag = tag + jnp.where(here & (sub == 0), clips[j], 0)
        tag = tag + jnp.where(here & (sub == 1), code, 0)
        tag = tag + jnp.where(sub == 2 + j, code, 0)
    tag = tag.astype(F32)
    mine[0, pair * blocks] = tag.astype(BF16)
    mine[1, pair * blocks] = tag.astype(BF16)
    for copy in takes[3:first]:
        copy.wait()
    pl.semaphore_wait(barrier, len(peers))

    def z_copy(q):
        return pltpu.make_async_remote_copy(
            mine.at[q % 2], near.at[q], s1.at[q], r1.at[q], device_id=z_peer(q), device_id_type=MESH)

    sent = []
    for q in z_steps:
        copy = z_copy(q)
        copy.start()
        sent.append(copy)

    def sort_in(sources, fresh):
        tags = [source[pair * blocks].astype(F32) for source in sources]
        codes = [
            (source, j, jnp.broadcast_to(words[2 + j : 3 + j, :], (share, 128)).astype(BF16))
            for source, words in zip(sources, tags) for j in range(blocks)
        ]
        for r in range(across):
            for h in range(pair):
                at = pl.ds(h * both, both)
                held = jnp.zeros((both, share, 128), BF16) if fresh else frame[r, at]
                for source, j, code in codes:
                    held = jnp.where(wanted[r] == code[None], source[h * blocks + j][None], held)
                frame[r, at] = held
        return sum(tags[1:], tags[0])

    for copy in takes[first:]:
        copy.wait()
    a = we[...].astype(F32)
    a = a - jnp.mean(a, axis=1, keepdims=True)
    b = be[...]
    b = b - jnp.mean(b, axis=1, keepdims=True)
    sub16 = lax.broadcasted_iota(I32, (16, depth), 0)
    base[0:channels, :] = a
    base[channels : channels + 16, :] = jnp.where(sub16 == 0, b, 0.0)
    gram = lax.dot_general(
        base[...], base[...], (((1,), (1,)), ((), ())), precision=HIGH, preferred_element_type=F32
    ) * (1.0 / depth)
    for k in range(3):
        part = gram.astype(BF16)
        gram_out[k] = part
        gram = gram - part.astype(F32)
    for k, g in enumerate((gq, gk)):
        gain = jnp.concatenate([g[...], lane_swapped(g[...])], axis=1)
        hi, lo = halves(table[...] * gain)
        halved[k, 0:128, :] = hi
        halved[k, 128:256, :] = lo

    z_copy(1).wait_recv()
    total = sort_in([mine.at[0], near.at[1]], True)
    for r in range(1, deep // 2 + 1):
        for q in sorted({2 * r, 2 * r + 1, 2 * (deep - r), 2 * (deep - r) + 1}):
            z_copy(q).wait_recv()
        for r_one in sorted({r, deep - r}):
            total = total + sort_in([near.at[2 * r_one], near.at[2 * r_one + 1]], False)
    for r in y_steps:
        frame[r, pair * both] = total.astype(BF16)

    def y_copy(r):
        return pltpu.make_async_remote_copy(
            frame.at[r], side.at[r], s2.at[r], r2.at[r], device_id=y_peer(r), device_id_type=MESH)

    for r in y_steps:
        copy = y_copy(r)
        copy.start()
        sent.append(copy)
    whole = frame[0, 0 : pair * both]
    for r in reversed(y_steps):
        y_copy(r).wait_recv()
        whole = whole + side[r, 0 : pair * both]
        total = total + side[r, pair * both].astype(F32)
    for c in range(2):
        for h in range(pair):
            ready[c, h * own : (h + 1) * own] = whole[h * both + c * own : h * both + (c + 1) * own]
    spot = 2 * x + core

    def x_copy(q):
        return pltpu.make_async_remote_copy(
            ready.at[(core + q) % 2], xt.at[spot], s3.at[q], r3.at[q], device_id=x_peer(q), device_id_type=MESH)

    for q in x_steps:
        copy = x_copy(q)
        copy.start()
        sent.append(copy)
    xt[spot] = ready[core]
    total = total.astype(I32)

    clip_row = jnp.broadcast_to(total[0:1, :], (8, 128))
    found = jnp.broadcast_to(total[1:2, :], (8, 128)) == me * own + sub
    clip_at = jnp.sum(jnp.where(found, clip_row, 0), axis=1, keepdims=True)
    block_at = jnp.sum(jnp.where(found, lane, 0), axis=1, keepdims=True)
    used_at = jnp.sum(jnp.where(found, 1, 0), axis=1, keepdims=True)
    earlier = jnp.sum(jnp.where(clip_row < clip_at, 1, 0), axis=1, keepdims=True)
    offset_at = (block_at - earlier) * tokens
    use[...] = jnp.broadcast_to(used_at.astype(F32), (8, 128))
    count = shift.shape[0]
    among = lax.broadcasted_iota(I32, (8, count), 1) == clip_at
    high_at = jnp.sum(jnp.where(among, extents[0:1, :], 0), axis=1, keepdims=True).astype(F32)
    wide_at = jnp.sum(jnp.where(among, extents[1:2, :], 0), axis=1, keepdims=True).astype(F32)
    pick = jnp.where(among, 1.0, 0.0).astype(BF16)
    moves = jnp.dot(pick, shift[...], preferred_element_type=F32)
    gains = 1.0 + jnp.dot(pick, scale[...], preferred_element_type=F32)
    sub8 = lax.broadcasted_iota(I32, (8, depth), 0)
    extra = []
    for s in range(own):
        gain = gains[s : s + 1, :]
        left[s * channels : (s + 1) * channels, :] = (base[0:channels, :] * gain).astype(BF16)
        middle = base[channels : channels + 1, :] * gain
        extra.append(jnp.where(sub8 == 0, middle, jnp.where(sub8 <= 2, moves[s : s + 1, :], 0.0)))
    left[own * channels :, :] = jnp.concatenate(extra, axis=0).astype(BF16)
    for copy in weights:
        copy.wait()

    def project(n, carry):
        m_out[n] = jnp.dot(left[...], w[n], preferred_element_type=F32)
        m_out[n + per] = jnp.dot(left[...], w[n + per], preferred_element_type=F32)
        return carry

    lax.fori_loop(0, per, project, 0)

    lane_f = lax.broadcasted_iota(I32, (1, 128), 1).astype(F32)
    steps = lax.broadcasted_iota(I32, (tokens, 128), 0).astype(F32)
    for s in range(own):
        high, wide = high_at[s : s + 1, :], wide_at[s : s + 1, :]
        high, wide = jnp.maximum(high, 1.0), jnp.maximum(wide, 1.0)
        index = offset_at[s : s + 1, :].astype(F32) + steps
        frames = jnp.floor((index + 0.5) * (1.0 / (high * wide)))
        lines = jnp.floor((index + 0.5) * (1.0 / wide))
        place = jnp.where(
            lane_f < 32.0, frames,
            jnp.where(lane_f < 80.0, lines - high * frames + 32.0, index - wide * lines + 80.0),
        )
        hot = jnp.where(place == lane_f, 1.0, 0.0).astype(BF16)
        hot = jnp.concatenate([hot, hot], axis=1)
        cs[0, s] = jnp.dot(hot, halved[0], preferred_element_type=F32)
        cs[1, s] = jnp.dot(hot, halved[1], preferred_element_type=F32)

    for q in reversed(x_steps):
        at = xt.at[(x + heads - q // 2) % heads * 2 + (core + q) % 2]
        pltpu.make_async_remote_copy(
            at, at, s3.at[q], r3.at[q], device_id=x_peer(q), device_id_type=MESH).wait_recv()
    for copy in sent:
        copy.wait_send()


def routed(
    across, clips, owners, slot_ids, latents, extents, we, be, shift, scale, gq, gk, wq, wk
):
    blocks, channels, tokens = latents.shape
    own = 2 * blocks
    heads, deep = lax.axis_size("head"), lax.axis_size("seq") // (2 * across)
    share, pair = channels // (2 * heads), tokens // 128
    both = 2 * own
    depth, columns = wq.shape
    chunks = 2 * columns // WIDE
    dma, room = pltpu.SemaphoreType.DMA, pltpu.VMEM
    table = jnp.asarray(rope_table())
    flat = [v.reshape(1, -1) for v in (be, gq, gk)]
    rows = own * (channels + 8)
    args = (clips, owners, slot_ids, latents, extents.T, we, flat[0], shift, scale, flat[1], flat[2], table, wq, wk)
    return pl.pallas_call(
        functools.partial(routing_kernel, deep=deep, across=across),
        out_shape=[
            jax.ShapeDtypeStruct((2 * heads, pair * own, share, 128), BF16),
            jax.ShapeDtypeStruct((chunks, rows, WIDE), F32),
            jax.ShapeDtypeStruct((2, own, tokens, 256), F32),
            jax.ShapeDtypeStruct((3, channels + 16, channels + 16), BF16),
            jax.ShapeDtypeStruct((8, 128), F32),
        ],
        in_specs=[HBM] * len(args),
        out_specs=[VMEM] * 5,
        scratch_shapes=[
            pltpu.SMEM(clips.shape, I32), pltpu.SMEM(clips.shape, I32), pltpu.SMEM(clips.shape, I32),
            *(room(v.shape, v.dtype) for v in (args[4], we, flat[0], shift, scale, flat[1], flat[2], table)),
            room((chunks, depth, WIDE), BF16),
            room((rows, depth), BF16),
            room((channels + 16, depth), F32),
            room((2, 256, 256), BF16),
            room((2, pair * blocks + 1, share, 128), BF16),
            room((2 * deep, pair * blocks + 1, share, 128), BF16),
            room((across, pair * both + 1, share, 128), BF16),
            room((across, both, share, 128), BF16),
            room((across, pair * both + 1, share, 128), BF16),
            room((2, pair * own, share, 128), BF16),
            dma((11 + 2 * pair,)), dma((chunks,)),
            dma((2 * deep,)), dma((2 * deep,)), dma((across,)), dma((across,)), dma((2 * heads,)), dma((2 * heads,)),
        ],
        compiler_params=pltpu.CompilerParams(
            collective_id=0, has_side_effects=True, vmem_limit_bytes=28 << 20),
        name="routing",
    )(*(pltpu.with_memory_space_constraint(v, pltpu.HBM) for v in args))


def finish_kernel(xt, m_in, cs, gram, use, oq, ok, zz, eps, out, o_sem):
    parts, both, share, _ = xt.shape
    slots, tokens = zz.shape[:2]
    pair = both // slots
    channels = parts * share
    chunks, _, wide = m_in.shape
    per = chunks // 2
    sub = lax.broadcasted_iota(I32, (16, tokens), 0)
    e_row = lax.broadcasted_iota(I32, (128, 128), 0)
    spread = jnp.where((e_row == channels + 3) | (e_row == channels + 4), 1.0, 0.0).astype(BF16)
    for s in range(slots):
        xf = jnp.concatenate(
            [jnp.concatenate([xt[p, h * slots + s].astype(F32) for h in range(pair)], axis=1)
             for p in range(parts)], axis=0)
        x1f = jnp.concatenate([xf, jnp.where(sub == 0, 1.0, 0.0)], axis=0)
        x1 = x1f.astype(BF16)
        y = sum(jnp.dot(gram[k], x1, preferred_element_type=F32) for k in range(3))
        var = jnp.maximum(jnp.sum(y * x1f, axis=0, keepdims=True), 0.0) + 1e-06
        dev = jnp.sqrt(var)
        dev_hi = dev.astype(BF16).astype(F32)
        small = var * 1e-06
        small_hi = small.astype(BF16).astype(F32)
        live = jnp.concatenate([use[s : s + 1, :]] * (tokens // 128), axis=1)
        more = jnp.where(
            sub == 0, live,
            jnp.where(sub == 1, dev_hi * live,
                      jnp.where(sub == 2, (dev - dev_hi) * live,
                                jnp.where(sub == 3, small_hi, jnp.where(sub == 4, small - small_hi, 0.0)))),
        )
        zt = jnp.concatenate([xf, more, jnp.zeros((112 - channels, tokens), F32)], axis=0)
        z = zt.astype(BF16).T
        eps[s] = jnp.dot(z, spread, preferred_element_type=F32)
        zz[s] = jnp.concatenate([z, z], axis=1)

    r_i = lax.broadcasted_iota(I32, (wide, wide), 0) // 128
    c_i = lax.broadcasted_iota(I32, (wide, wide), 1) // 128
    ones = jnp.where(r_i == c_i, 1.0 / 128.0, 0.0).astype(BF16)
    empty = jnp.zeros((128 - channels - 8, wide), F32)

    def stack(m, s):
        own = jnp.concatenate(
            [m[s * channels : (s + 1) * channels],
             m[slots * channels + 8 * s : slots * channels + 8 * s + 8], empty], axis=0)
        hi, lo = halves(own)
        return jnp.concatenate([hi, lo], axis=0)

    def out_copy(n, place):
        return pltpu.make_async_copy(
            out.at[n], place.at[:, pl.ds(n % per * wide, wide)], o_sem.at[n])

    def chunk(n):
        m = m_in[n]
        turned = lane_swapped(m)
        for s in range(slots):
            z = zz[s]
            v = jnp.dot(z, stack(m, s), preferred_element_type=F32)
            vs = jnp.dot(z, stack(turned, s), preferred_element_type=F32)
            power = jnp.dot((v * v).astype(BF16), ones, preferred_element_type=F32)
            c = cs[n // per, s, :, 0:128]
            sn = cs[n // per, s, :, 128:256]
            e = eps[s]
            for h in range(wide // 128):
                at = slice(h * 128, (h + 1) * 128)
                o = (v[:, at] * c + vs[:, at] * sn) * lax.rsqrt(power[:, at] + e)
                out[n, s * tokens : (s + 1) * tokens, at] = o.astype(BF16)
        out_copy(n, oq if n < per else ok).start()

    for n in range(chunks):
        chunk(n)
    for n in range(chunks):
        out_copy(n, oq if n < per else ok).wait()


def finished(xt, m, cs, gram, use):
    slots, tokens = cs.shape[1:3]
    chunks, _, wide = m.shape
    rows = slots * tokens
    return pl.pallas_call(
        finish_kernel,
        out_shape=[jax.ShapeDtypeStruct((rows, chunks // 2 * wide), BF16)] * 2,
        in_specs=[VMEM] * 5,
        out_specs=[pl.BlockSpec(memory_space=pl.ANY)] * 2,
        scratch_shapes=[
            pltpu.VMEM((slots, tokens, 256), BF16),
            pltpu.VMEM((slots, tokens, 128), F32),
            pltpu.VMEM((chunks, rows, wide), BF16),
            pltpu.SemaphoreType.DMA((chunks,)),
        ],
        compiler_params=pltpu.CompilerParams(vmem_limit_bytes=28 << 20),
        name="finish",
    )(xt, m, cs, gram, use)


def per_device(
    across, latents, clip_ids, owners, slots, extents, embed_weight, embed_bias, shift_table, scale_table,
    query_weight, key_weight, query_gain, key_gain,
):
    parts = routed(
        across, clip_ids, owners, slots, jnp.transpose(latents, (0, 2, 1)), extents, embed_weight, embed_bias,
        shift_table, scale_table, query_gain, key_gain, query_weight, key_weight,
    )
    return tuple(finished(*parts))


def solution(mesh):
    placed = (
        P("seq", None, None),
        P("seq"),
        P("seq"),
        P("seq"),
        P(),
        P(),
        P(),
        P(),
        P(),
        P(None, "head"),
        P(None, "head"),
        P(),
        P(),
    )
    return jax.shard_map(
        functools.partial(per_device, 4),
        mesh=mesh,
        in_specs=placed,
        out_specs=(P("seq", "head"), P("seq", "head")),
        check_vma=False,
    )
```

```python
import functools
import jax
import jax.numpy as jnp
import numpy as np
from jax import lax
from jax.experimental import pallas as pl
from jax.experimental.pallas import tpu as pltpu
from jax.sharding import PartitionSpec as P

F32, BF16, I32 = jnp.float32, jnp.bfloat16, jnp.int32
HIGH = lax.Precision.HIGHEST
MESH = pl.DeviceIdType.MESH
WIDE = 256
HBM = pl.BlockSpec(memory_space=pltpu.HBM)
VMEM = pl.BlockSpec(memory_space=pltpu.VMEM)


def rope_table():
    table = np.zeros((128, 256), np.float32)
    row = lane = 0
    for places, width in ((32, 16), (48, 56), (48, 56)):
        rate = 1.0 / 10000.0 ** (np.arange(0, width, 2, dtype=np.float32) / np.float32(width))
        angle = np.arange(places, dtype=np.float32)[:, None] * rate[None, :].astype(np.float32)
        span = slice(lane, lane + width)
        table[row : row + places, span] = np.repeat(np.cos(angle), 2, axis=1)
        sines = np.repeat(np.sin(angle), 2, axis=1)
        sines[:, 0::2] *= -1.0
        table[row : row + places, 128 + lane : 128 + lane + width] = sines
        row, lane = row + places, lane + width
    return table


def lane_swapped(x):
    width = x.shape[-1]
    even = lax.broadcasted_iota(I32, x.shape, 1) % 2 == 0
    return jnp.where(even, pltpu.roll(x, width - 1, 1), pltpu.roll(x, 1, 1))


def halves(x):
    top = x.astype(BF16)
    return top, (x - top.astype(F32)).astype(BF16)


def routing_kernel(
    clips_h, owners_h, slots_h, latents, extents_h, we_h, be_h, shift_h, scale_h, gq_h, gk_h, table_h, wq, wk,
    xt, stacks, cs, gram_out, use,
    clips, owners, slot_ids, extents, we, be, shift, scale, gq, gk, table, w, left, held, base, halved,
    mine, near, frame, wanted, side, ready,
    in_sem, w_sem, s1, r1, s2, r2, s3, r3,
    *, deep, across,
):
    me = lax.axis_index("seq")
    x = lax.axis_index("head")
    heads = xt.shape[0] // 2
    blocks, channels, tokens = latents.shape
    share = channels // (2 * heads)
    pair = tokens // 128
    group = 2 * across
    plane, y, core = me // group, me % group // 2, me % 2
    own = 2 * blocks
    both = 2 * own
    depth = we_h.shape[1]
    per = w.shape[0] // 2

    def z_peer(q):
        return {"seq": ((plane + q // 2) % deep * across + y) * 2 + (core + q) % 2}

    def y_peer(r):
        return {"seq": (plane * across + (y + r) % across) * 2 + core}

    def x_peer(q):
        return {"seq": me - core + (core + q) % 2, "head": (x + q // 2) % heads}

    z_steps = sorted(range(1, 2 * deep), key=lambda q: -min(q // 2, deep - q // 2))
    y_steps = sorted(range(1, across), key=lambda r: -min(r, across - r))
    x_steps = sorted(range(1, 2 * heads), key=lambda q: -min(q // 2, heads - q // 2))
    first = 3 + 2 * pair
    takes = [
        pltpu.make_async_copy(source, place, in_sem.at[k])
        for k, (source, place) in enumerate((
            (clips_h, clips), (owners_h, owners), (slots_h, slot_ids),
            *((latents.at[:, pl.ds(pl.multiple_of((2 * x + (core + k) % 2) * share, share), share),
                          h * 128 : (h + 1) * 128],
               mine.at[k, h * blocks : (h + 1) * blocks]) for k in range(2) for h in range(pair)),
            (we_h, we), (be_h, be), (gq_h, gq), (gk_h, gk), (table_h, table),
            (shift_h, shift), (scale_h, scale), (extents_h, extents),
        ))
    ]
    weights = [
        pltpu.make_async_copy(source.at[:, pl.ds(n * WIDE, WIDE)], w.at[k * per + n], w_sem.at[k * per + n])
        for n in range(per) for k, source in enumerate((wq, wk))
    ]
    for copy in takes[:first]:
        copy.start()
    peers = [z_peer(q) for q in z_steps] + [y_peer(r) for r in y_steps] + [x_peer(q) for q in x_steps if q != 1]
    barrier = pltpu.get_barrier_semaphore()
    for peer in peers:
        pl.semaphore_signal(barrier, inc=1, device_id=peer, device_id_type=MESH)

    sub = lax.broadcasted_iota(I32, (8, 128), 0)
    lane = lax.broadcasted_iota(I32, (8, 128), 1)
    for copy in takes[:3]:
        copy.wait()
    tag = jnp.zeros((8, 128), I32)
    for j in range(blocks):
        code = owners[j] * own + slot_ids[j]
        here = lane == blocks * me + j
        tag = tag + jnp.where(here & (sub == 0), clips[j], 0)
        tag = tag + jnp.where(here & (sub == 1), code, 0)
        tag = tag + jnp.where(sub == 2 + j, code, 0)
    tag = tag.astype(F32)
    mine[0, pair * blocks] = tag.astype(BF16)
    mine[1, pair * blocks] = tag.astype(BF16)
    for copy in takes[3:first]:
        copy.wait()
    pl.semaphore_wait(barrier, len(peers))

    def z_copy(q):
        return pltpu.make_async_remote_copy(
            mine.at[q % 2], near.at[q], s1.at[q], r1.at[q], device_id=z_peer(q), device_id_type=MESH)

    sent = []
    for q in z_steps:
        copy = z_copy(q)
        copy.start()
        sent.append(copy)

    for copy in takes[first:] + weights:
        copy.start()
    for r in range(across):
        for s in range(both):
            code = (plane * across + (y + r) % across) * both + s
            wanted[r, s] = jnp.full((share, 128), code, I32).astype(F32).astype(BF16)

    def sort_in(sources, fresh):
        tags = [source[pair * blocks].astype(F32) for source in sources]
        codes = [
            (source, j, jnp.broadcast_to(words[2 + j : 3 + j, :], (share, 128)).astype(BF16))
            for source, words in zip(sources, tags) for j in range(blocks)
        ]
        for r in range(across):
            for h in range(pair):
                at = pl.ds(h * both, both)
                held = jnp.zeros((both, share, 128), BF16) if fresh else frame[r, at]
                for source, j, code in codes:
                    held = jnp.where(wanted[r] == code[None], source[h * blocks + j][None], held)
                frame[r, at] = held
        return sum(tags[1:], tags[0])

    for copy in takes[first:]:
        copy.wait()
    a = we[...].astype(F32)
    a = a - jnp.mean(a, axis=1, keepdims=True)
    b = be[...]
    b = b - jnp.mean(b, axis=1, keepdims=True)
    sub16 = lax.broadcasted_iota(I32, (16, depth), 0)
    base[0:channels, :] = a
    base[channels : channels + 16, :] = jnp.where(sub16 == 0, b, 0.0)
    gram = lax.dot_general(
        base[...], base[...], (((1,), (1,)), ((), ())), precision=HIGH, preferred_element_type=F32
    ) * (1.0 / depth)
    for k in range(3):
        part = gram.astype(BF16)
        gram_out[k] = part
        gram = gram - part.astype(F32)
    for k, g in enumerate((gq, gk)):
        gain = jnp.concatenate([g[...], lane_swapped(g[...])], axis=1)
        hi, lo = halves(table[...] * (gain * 128.0**0.5))
        halved[k, 0:128, :] = hi
        halved[k, 128:256, :] = lo

    z_copy(1).wait_recv()
    total = sort_in([mine.at[0], near.at[1]], True)
    for r in range(1, deep // 2 + 1):
        for q in sorted({2 * r, 2 * r + 1, 2 * (deep - r), 2 * (deep - r) + 1}):
            z_copy(q).wait_recv()
        for r_one in sorted({r, deep - r}):
            total = total + sort_in([near.at[2 * r_one], near.at[2 * r_one + 1]], False)
    for r in y_steps:
        frame[r, pair * both] = total.astype(BF16)

    def y_copy(r):
        return pltpu.make_async_remote_copy(
            frame.at[r], side.at[r], s2.at[r], r2.at[r], device_id=y_peer(r), device_id_type=MESH)

    for r in y_steps:
        copy = y_copy(r)
        copy.start()
        sent.append(copy)
    whole = frame[0, 0 : pair * both]
    for r in reversed(y_steps):
        y_copy(r).wait_recv()
        whole = whole + side[r, 0 : pair * both]
        total = total + side[r, pair * both].astype(F32)
    for c in range(2):
        for h in range(pair):
            ready[c, h * own : (h + 1) * own] = whole[h * both + c * own : h * both + (c + 1) * own]
    spot = 2 * x + core

    def x_copy(q):
        return pltpu.make_async_remote_copy(
            ready.at[(core + q) % 2], xt.at[spot], s3.at[q], r3.at[q], device_id=x_peer(q), device_id_type=MESH)

    for q in x_steps:
        copy = x_copy(q)
        copy.start()
        sent.append(copy)
    xt[spot] = ready[core]
    total = total.astype(I32)

    clip_row = jnp.broadcast_to(total[0:1, :], (8, 128))
    found = jnp.broadcast_to(total[1:2, :], (8, 128)) == me * own + sub
    clip_at = jnp.sum(jnp.where(found, clip_row, 0), axis=1, keepdims=True)
    block_at = jnp.sum(jnp.where(found, lane, 0), axis=1, keepdims=True)
    used_at = jnp.sum(jnp.where(found, 1, 0), axis=1, keepdims=True)
    earlier = jnp.sum(jnp.where(clip_row < clip_at, 1, 0), axis=1, keepdims=True)
    offset_at = (block_at - earlier) * tokens
    use[...] = jnp.broadcast_to(used_at.astype(F32), (8, 128))
    count = shift.shape[0]
    among = lax.broadcasted_iota(I32, (8, count), 1) == clip_at
    high_at = jnp.sum(jnp.where(among, extents[0:1, :], 0), axis=1, keepdims=True).astype(F32)
    wide_at = jnp.sum(jnp.where(among, extents[1:2, :], 0), axis=1, keepdims=True).astype(F32)
    pick = jnp.where(among, 1.0, 0.0).astype(BF16)
    moves = jnp.dot(pick, shift[...], preferred_element_type=F32)
    gains = 1.0 + jnp.dot(pick, scale[...], preferred_element_type=F32)
    sub8 = lax.broadcasted_iota(I32, (8, depth), 0)
    extra = []
    for s in range(own):
        gain = gains[s : s + 1, :]
        left[s * channels : (s + 1) * channels, :] = (base[0:channels, :] * gain).astype(BF16)
        middle = base[channels : channels + 1, :] * gain
        extra.append(jnp.where((sub8 == 0) | (sub8 == 3), middle, jnp.where(sub8 <= 4, moves[s : s + 1, :], 0.0)))
    left[own * channels :, :] = jnp.concatenate(extra, axis=0).astype(BF16)
    for copy in weights:
        copy.wait()

    late = lax.broadcasted_iota(I32, (16, WIDE), 0) >= 3
    blank = jnp.zeros((8, WIDE), F32)

    def place(m, n, k):
        hi, lo = halves(m[0 : own * channels])
        for s in range(own):
            rows = slice(s * channels, (s + 1) * channels)
            stacks[n, s, k, 0:channels, :] = hi[rows]
            stacks[n, s, k, channels : 2 * channels, :] = lo[rows]
            tail = jnp.concatenate([m[own * channels + 8 * s : own * channels + 8 * s + 8], blank], axis=0)
            over = tail - tail.astype(BF16).astype(F32)
            stacks[n, s, k, 2 * channels :, :] = jnp.where(late, over, tail).astype(BF16)

    def products(n):
        for k in range(2):
            held[k] = jnp.dot(left[...], w[n + k * per], preferred_element_type=F32)

    def placed(n):
        for k in range(2):
            m = held[k]
            place(m, n + k * per, 0)
            place(lane_swapped(m), n + k * per, 1)

    def both_at(n, carry):
        placed((n + per - 1) % per)
        products(n)
        return carry

    held[...] = jnp.zeros_like(held)
    lax.fori_loop(0, per, both_at, 0)
    placed(per - 1)

    lane_f = lax.broadcasted_iota(I32, (1, 128), 1).astype(F32)
    steps = lax.broadcasted_iota(I32, (tokens, 128), 0).astype(F32)
    for s in range(own):
        high, wide = high_at[s : s + 1, :], wide_at[s : s + 1, :]
        high, wide = jnp.maximum(high, 1.0), jnp.maximum(wide, 1.0)
        index = offset_at[s : s + 1, :].astype(F32) + steps
        frames = jnp.floor((index + 0.5) * (1.0 / (high * wide)))
        lines = jnp.floor((index + 0.5) * (1.0 / wide))
        place = jnp.where(
            lane_f < 32.0, frames,
            jnp.where(lane_f < 80.0, lines - high * frames + 32.0, index - wide * lines + 80.0),
        )
        hot = jnp.where(place == lane_f, 1.0, 0.0).astype(BF16)
        hot = jnp.concatenate([hot, hot], axis=1)
        cs[0, s] = jnp.dot(hot, halved[0], preferred_element_type=F32)
        cs[1, s] = jnp.dot(hot, halved[1], preferred_element_type=F32)

    for q in reversed(x_steps):
        at = xt.at[(x + heads - q // 2) % heads * 2 + (core + q) % 2]
        pltpu.make_async_remote_copy(
            at, at, s3.at[q], r3.at[q], device_id=x_peer(q), device_id_type=MESH).wait_recv()
    for copy in sent:
        copy.wait_send()


def routed(
    across, clips, owners, slot_ids, latents, extents, we, be, shift, scale, gq, gk, wq, wk
):
    blocks, channels, tokens = latents.shape
    own = 2 * blocks
    heads, deep = lax.axis_size("head"), lax.axis_size("seq") // (2 * across)
    share, pair = channels // (2 * heads), tokens // 128
    both = 2 * own
    depth, columns = wq.shape
    chunks = 2 * columns // WIDE
    dma, room = pltpu.SemaphoreType.DMA, pltpu.VMEM
    table = jnp.asarray(rope_table())
    flat = [v.reshape(1, -1) for v in (be, gq, gk)]
    rows = own * (channels + 8)
    args = (clips, owners, slot_ids, latents, extents.T, we, flat[0], shift, scale, flat[1], flat[2], table, wq, wk)
    return pl.pallas_call(
        functools.partial(routing_kernel, deep=deep, across=across),
        out_shape=[
            jax.ShapeDtypeStruct((2 * heads, pair * own, share, 128), BF16),
            jax.ShapeDtypeStruct((chunks, own, 2, 2 * channels + 16, WIDE), BF16),
            jax.ShapeDtypeStruct((2, own, tokens, 256), F32),
            jax.ShapeDtypeStruct((3, channels + 16, channels + 16), BF16),
            jax.ShapeDtypeStruct((8, 128), F32),
        ],
        in_specs=[HBM] * len(args),
        out_specs=[VMEM] * 5,
        scratch_shapes=[
            pltpu.SMEM(clips.shape, I32), pltpu.SMEM(clips.shape, I32), pltpu.SMEM(clips.shape, I32),
            *(room(v.shape, v.dtype) for v in (args[4], we, flat[0], shift, scale, flat[1], flat[2], table)),
            room((chunks, depth, WIDE), BF16),
            room((rows, depth), BF16),
            room((2, rows, WIDE), F32),
            room((channels + 16, depth), F32),
            room((2, 256, 256), BF16),
            room((2, pair * blocks + 1, share, 128), BF16),
            room((2 * deep, pair * blocks + 1, share, 128), BF16),
            room((across, pair * both + 1, share, 128), BF16),
            room((across, both, share, 128), BF16),
            room((across, pair * both + 1, share, 128), BF16),
            room((2, pair * own, share, 128), BF16),
            dma((11 + 2 * pair,)), dma((chunks,)),
            dma((2 * deep,)), dma((2 * deep,)), dma((across,)), dma((across,)), dma((2 * heads,)), dma((2 * heads,)),
        ],
        compiler_params=pltpu.CompilerParams(
            collective_id=0, has_side_effects=True, vmem_limit_bytes=28 << 20),
        name="routing",
    )(*(pltpu.with_memory_space_constraint(v, pltpu.HBM) for v in args))


def finish_kernel(xt, stacks, cs, gram, use, oq, ok, zz, eps, out, o_sem):
    parts, both, share, _ = xt.shape
    slots, tokens = zz.shape[:2]
    pair = both // slots
    channels = parts * share
    chunks, _, _, deep, wide = stacks.shape
    per = chunks // 2
    sub = lax.broadcasted_iota(I32, (16, tokens), 0)
    e_row = lax.broadcasted_iota(I32, (deep, 128), 0)
    spread = jnp.where(e_row // 2 == channels + 3, 1.0, 0.0).astype(BF16)
    for s in range(slots):
        xf = jnp.concatenate(
            [jnp.concatenate([xt[p, h * slots + s].astype(F32) for h in range(pair)], axis=1)
             for p in range(parts)], axis=0)
        x1f = jnp.concatenate([xf, jnp.where(sub == 0, 1.0, 0.0)], axis=0)
        x1 = x1f.astype(BF16)
        y = sum(jnp.dot(gram[k], x1, preferred_element_type=F32) for k in range(3))
        var = jnp.maximum(jnp.sum(y * x1f, axis=0, keepdims=True), 0.0) + 1e-06
        dev = jnp.sqrt(var)
        dev_hi = dev.astype(BF16).astype(F32)
        small = var * (128.0 * 1e-06)
        small_hi = small.astype(BF16).astype(F32)
        live = jnp.concatenate([use[s : s + 1, :]] * (tokens // 128), axis=1)
        more = jnp.where((sub == 1) | (sub == 4), dev_hi, jnp.where(sub == 2, dev - dev_hi, 1.0)) * live
        more = jnp.where(sub < 5, more, jnp.where(sub == 6, small_hi, jnp.where(sub == 7, small - small_hi, 0.0)))
        zt = jnp.concatenate([xf, xf, more], axis=0)
        z = zt.astype(BF16).T
        eps[s] = jnp.dot(z, spread, preferred_element_type=F32)
        zz[s] = z

    def out_copy(n, place):
        return pltpu.make_async_copy(
            out.at[n], place.at[:, pl.ds(n % per * wide, wide)], o_sem.at[n])

    def chunk(n):
        for s in range(slots):
            z = zz[s]
            v = jnp.dot(z, stacks[n, s, 0], preferred_element_type=F32)
            vs = jnp.dot(z, stacks[n, s, 1], preferred_element_type=F32)
            c = cs[n // per, s, :, 0:128]
            sn = cs[n // per, s, :, 128:256]
            e = eps[s]
            for h in range(wide // 128):
                at = slice(h * 128, (h + 1) * 128)
                power = jnp.sum(v[:, at] * v[:, at], axis=1, keepdims=True)
                o = (v[:, at] * c + vs[:, at] * sn) * lax.rsqrt(power + e)
                out[n, s * tokens : (s + 1) * tokens, at] = o.astype(BF16)
        out_copy(n, oq if n < per else ok).start()

    for n in range(chunks):
        chunk(n)
    for n in range(chunks):
        out_copy(n, oq if n < per else ok).wait()


def finished(xt, stacks, cs, gram, use):
    slots, tokens = cs.shape[1:3]
    chunks, _, _, deep, wide = stacks.shape
    rows = slots * tokens
    return pl.pallas_call(
        finish_kernel,
        out_shape=[jax.ShapeDtypeStruct((rows, chunks // 2 * wide), BF16)] * 2,
        in_specs=[VMEM] * 5,
        out_specs=[pl.BlockSpec(memory_space=pl.ANY)] * 2,
        scratch_shapes=[
            pltpu.VMEM((slots, tokens, deep), BF16),
            pltpu.VMEM((slots, tokens, 128), F32),
            pltpu.VMEM((chunks, rows, wide), BF16),
            pltpu.SemaphoreType.DMA((chunks,)),
        ],
        compiler_params=pltpu.CompilerParams(vmem_limit_bytes=28 << 20),
        name="finish",
    )(xt, stacks, cs, gram, use)


def per_device(
    across, latents, clip_ids, owners, slots, extents, embed_weight, embed_bias, shift_table, scale_table,
    query_weight, key_weight, query_gain, key_gain,
):
    parts = routed(
        across, clip_ids, owners, slots, jnp.transpose(latents, (0, 2, 1)), extents, embed_weight, embed_bias,
        shift_table, scale_table, query_gain, key_gain, query_weight, key_weight,
    )
    return tuple(finished(*parts))


def solution(mesh):
    placed = (
        P("seq", None, None),
        P("seq"),
        P("seq"),
        P("seq"),
        P(),
        P(),
        P(),
        P(),
        P(),
        P(None, "head"),
        P(None, "head"),
        P(),
        P(),
    )
    return jax.shard_map(
        functools.partial(per_device, 4),
        mesh=mesh,
        in_specs=placed,
        out_specs=(P("seq", "head"), P("seq", "head")),
        check_vma=False,
    )
```

```python
import functools
import jax
import jax.numpy as jnp
import numpy as np
from jax import lax
from jax.experimental import pallas as pl
from jax.experimental.pallas import tpu as pltpu
from jax.sharding import PartitionSpec as P

F32, BF16, I32 = jnp.float32, jnp.bfloat16, jnp.int32
HIGH = lax.Precision.HIGHEST
MESH = pl.DeviceIdType.MESH
WIDE = 256
HBM = pl.BlockSpec(memory_space=pltpu.HBM)
VMEM = pl.BlockSpec(memory_space=pltpu.VMEM)


def rope_table():
    table = np.zeros((128, 256), np.float32)
    row = lane = 0
    for places, width in ((32, 16), (48, 56), (48, 56)):
        rate = 1.0 / 10000.0 ** (np.arange(0, width, 2, dtype=np.float32) / np.float32(width))
        angle = np.arange(places, dtype=np.float32)[:, None] * rate[None, :].astype(np.float32)
        span = slice(lane, lane + width)
        table[row : row + places, span] = np.repeat(np.cos(angle), 2, axis=1)
        sines = np.repeat(np.sin(angle), 2, axis=1)
        sines[:, 0::2] *= -1.0
        table[row : row + places, 128 + lane : 128 + lane + width] = sines
        row, lane = row + places, lane + width
    return table


def lane_swapped(x):
    width = x.shape[-1]
    even = lax.broadcasted_iota(I32, x.shape, 1) % 2 == 0
    return jnp.where(even, pltpu.roll(x, width - 1, 1), pltpu.roll(x, 1, 1))


def halves(x):
    top = x.astype(BF16)
    return top, (x - top.astype(F32)).astype(BF16)


def routing_kernel(
    clips_h, owners_h, slots_h, latents, extents_h, we_h, be_h, shift_h, scale_h, gq_h, gk_h, table_h, wq, wk,
    xt, stacks, cs, gram_out, use,
    clips, owners, slot_ids, extents, we, be, shift, scale, gq, gk, table, w, left, held, base, halved,
    mine, near, frame, wanted, side, ready,
    in_sem, w_sem, s1, r1, s2, r2, s3, r3,
    *, deep, across,
):
    me = lax.axis_index("seq")
    x = lax.axis_index("head")
    heads = xt.shape[0] // 2
    blocks, channels, tokens = latents.shape
    share = channels // (2 * heads)
    pair = tokens // 128
    group = 2 * across
    div, rem = lax.div, lax.rem
    plane, y, core = div(me, group), div(rem(me, group), 2), rem(me, 2)
    other = 1 - core
    own = 2 * blocks
    both = 2 * own
    depth = we_h.shape[1]
    per = w.shape[0] // 2

    def z_peer(q):
        return {"seq": (rem(plane + q // 2, deep) * across + y) * 2 + (other if q % 2 else core)}

    def y_peer(r):
        return {"seq": (plane * across + rem(y + r, across)) * 2 + core}

    def x_peer(q):
        return {"seq": me - core + (other if q % 2 else core), "head": rem(x + q // 2, heads)}

    z_steps = sorted(range(1, 2 * deep), key=lambda q: -min(q // 2, deep - q // 2))
    y_steps = sorted(range(1, across), key=lambda r: -min(r, across - r))
    x_steps = sorted(range(1, 2 * heads), key=lambda q: -min(q // 2, heads - q // 2))
    peers = [z_peer(q) for q in z_steps] + [y_peer(r) for r in y_steps] + [x_peer(q) for q in x_steps if q != 1]
    barrier = pltpu.get_barrier_semaphore()
    for peer in peers:
        pl.semaphore_signal(barrier, inc=1, device_id=peer, device_id_type=MESH)
    first = 3 + 2 * pair
    takes = [
        pltpu.make_async_copy(source, place, in_sem.at[k])
        for k, (source, place) in enumerate((
            (clips_h, clips), (owners_h, owners), (slots_h, slot_ids),
            *((latents.at[:, pl.ds(pl.multiple_of((2 * x + (other if k else core)) * share, share), share),
                          h * 128 : (h + 1) * 128],
               mine.at[k, h * blocks : (h + 1) * blocks]) for k in range(2) for h in range(pair)),
            (we_h, we), (be_h, be), (gq_h, gq), (gk_h, gk), (table_h, table),
            (shift_h, shift), (scale_h, scale), (extents_h, extents),
        ))
    ]
    weights = [
        pltpu.make_async_copy(source.at[:, pl.ds(n * WIDE, WIDE)], w.at[k * per + n], w_sem.at[k * per + n])
        for n in range(per) for k, source in enumerate((wq, wk))
    ]
    for copy in takes[:first]:
        copy.start()

    sub = lax.broadcasted_iota(I32, (8, 128), 0)
    lane = lax.broadcasted_iota(I32, (8, 128), 1)
    for copy in takes[:3]:
        copy.wait()
    tag = jnp.zeros((8, 128), I32)
    for j in range(blocks):
        code = owners[j] * own + slot_ids[j]
        here = lane == blocks * me + j
        tag = tag + jnp.where(here & (sub == 0), clips[j], 0)
        tag = tag + jnp.where(here & (sub == 1), code, 0)
        tag = tag + jnp.where(sub == 2 + j, code, 0)
    tag = tag.astype(F32)
    mine[0, pair * blocks] = tag.astype(BF16)
    mine[1, pair * blocks] = tag.astype(BF16)
    for copy in takes[3:first]:
        copy.wait()
    pl.semaphore_wait(barrier, len(peers))

    def z_copy(q):
        return pltpu.make_async_remote_copy(
            mine.at[q % 2], near.at[q], s1.at[q], r1.at[q], device_id=z_peer(q), device_id_type=MESH)

    sent = []
    for q in z_steps:
        copy = z_copy(q)
        copy.start()
        sent.append(copy)

    for copy in takes[first:] + weights:
        copy.start()
    for r in range(across):
        for s in range(both):
            code = (plane * across + rem(y + r, across)) * both + s
            wanted[r, s] = jnp.full((share, 128), code, I32).astype(F32).astype(BF16)

    def sort_in(sources, fresh):
        tags = [source[pair * blocks].astype(F32) for source in sources]
        codes = [
            (source, j, jnp.broadcast_to(words[2 + j : 3 + j, :], (share, 128)).astype(BF16))
            for source, words in zip(sources, tags) for j in range(blocks)
        ]
        for r in range(across):
            for h in range(pair):
                at = pl.ds(h * both, both)
                held = jnp.zeros((both, share, 128), BF16) if fresh else frame[r, at]
                for source, j, code in codes:
                    held = jnp.where(wanted[r] == code[None], source[h * blocks + j][None], held)
                frame[r, at] = held
        return sum(tags[1:], tags[0])

    for copy in takes[first:]:
        copy.wait()
    a = we[...].astype(F32)
    a = a - jnp.mean(a, axis=1, keepdims=True)
    b = be[...]
    b = b - jnp.mean(b, axis=1, keepdims=True)
    sub16 = lax.broadcasted_iota(I32, (16, depth), 0)
    base[0:channels, :] = a
    base[channels : channels + 16, :] = jnp.where(sub16 == 0, b, 0.0)
    gram = lax.dot_general(
        base[...], base[...], (((1,), (1,)), ((), ())), precision=HIGH, preferred_element_type=F32
    ) * (1.0 / depth)
    for k in range(3):
        part = gram.astype(BF16)
        gram_out[k] = part
        gram = gram - part.astype(F32)
    for k, g in enumerate((gq, gk)):
        gain = jnp.concatenate([g[...], lane_swapped(g[...])], axis=1)
        hi, lo = halves(table[...] * (gain * 128.0**0.5))
        halved[k, 0:128, :] = hi
        halved[k, 128:256, :] = lo

    z_copy(1).wait_recv()
    total = sort_in([mine.at[0], near.at[1]], True)
    for r in range(1, deep // 2 + 1):
        for r_one in sorted({r, deep - r}, reverse=True):
            for q in (2 * r_one, 2 * r_one + 1):
                z_copy(q).wait_recv()
            total = total + sort_in([near.at[2 * r_one], near.at[2 * r_one + 1]], False)
    for r in y_steps:
        frame[r, pair * both] = total.astype(BF16)

    def y_copy(r):
        return pltpu.make_async_remote_copy(
            frame.at[r], side.at[r], s2.at[r], r2.at[r], device_id=y_peer(r), device_id_type=MESH)

    for r in y_steps:
        copy = y_copy(r)
        copy.start()
        sent.append(copy)
    whole = frame[0, 0 : pair * both]
    for r in reversed(y_steps):
        y_copy(r).wait_recv()
        whole = whole + side[r, 0 : pair * both]
        total = total + side[r, pair * both].astype(F32)
    for c in range(2):
        for h in range(pair):
            ready[c, h * own : (h + 1) * own] = whole[h * both + c * own : h * both + (c + 1) * own]
    spot = 2 * x + core

    def x_copy(q):
        return pltpu.make_async_remote_copy(
            ready.at[other if q % 2 else core], xt.at[spot], s3.at[q], r3.at[q], device_id=x_peer(q), device_id_type=MESH)

    for q in x_steps:
        copy = x_copy(q)
        copy.start()
        sent.append(copy)
    xt[spot] = ready[core]
    total = total.astype(I32)

    clip_row = jnp.broadcast_to(total[0:1, :], (8, 128))
    found = jnp.broadcast_to(total[1:2, :], (8, 128)) == me * own + sub
    clip_at = jnp.sum(jnp.where(found, clip_row, 0), axis=1, keepdims=True)
    block_at = jnp.sum(jnp.where(found, lane, 0), axis=1, keepdims=True)
    used_at = jnp.sum(jnp.where(found, 1, 0), axis=1, keepdims=True)
    earlier = jnp.sum(jnp.where(clip_row < clip_at, 1, 0), axis=1, keepdims=True)
    offset_at = (block_at - earlier) * tokens
    use[...] = jnp.broadcast_to(used_at.astype(F32), (8, 128))
    count = shift.shape[0]
    among = lax.broadcasted_iota(I32, (8, count), 1) == clip_at
    high_at = jnp.sum(jnp.where(among, extents[0:1, :], 0), axis=1, keepdims=True).astype(F32)
    wide_at = jnp.sum(jnp.where(among, extents[1:2, :], 0), axis=1, keepdims=True).astype(F32)
    pick = jnp.where(among, 1.0, 0.0).astype(BF16)
    moves = jnp.dot(pick, shift[...], preferred_element_type=F32)
    gains = 1.0 + jnp.dot(pick, scale[...], preferred_element_type=F32)
    sub8 = lax.broadcasted_iota(I32, (8, depth), 0)
    extra = []
    for s in range(own):
        gain = gains[s : s + 1, :]
        left[s * channels : (s + 1) * channels, :] = (base[0:channels, :] * gain).astype(BF16)
        middle = base[channels : channels + 1, :] * gain
        extra.append(jnp.where((sub8 == 0) | (sub8 == 3), middle, jnp.where(sub8 <= 4, moves[s : s + 1, :], 0.0)))
    left[own * channels :, :] = jnp.concatenate(extra, axis=0).astype(BF16)
    for copy in weights:
        copy.wait()

    late = lax.broadcasted_iota(I32, (16, WIDE), 0) >= 3
    blank = jnp.zeros((8, WIDE), F32)

    def place(m, n, k):
        hi, lo = halves(m[0 : own * channels])
        for s in range(own):
            rows = slice(s * channels, (s + 1) * channels)
            stacks[n, s, k, 0:channels, :] = hi[rows]
            stacks[n, s, k, channels : 2 * channels, :] = lo[rows]
            tail = jnp.concatenate([m[own * channels + 8 * s : own * channels + 8 * s + 8], blank], axis=0)
            over = tail - tail.astype(BF16).astype(F32)
            stacks[n, s, k, 2 * channels :, :] = jnp.where(late, over, tail).astype(BF16)

    def products(n):
        for k in range(2):
            held[k] = jnp.dot(left[...], w[n + k * per], preferred_element_type=F32)

    def placed(n):
        for k in range(2):
            m = held[k]
            place(m, n + k * per, 0)
            place(lane_swapped(m), n + k * per, 1)

    def both_at(n, carry):
        placed((n + per - 1) % per)
        products(n)
        return carry

    held[...] = jnp.zeros_like(held)
    lax.fori_loop(0, per, both_at, 0)
    placed(per - 1)

    lane_f = lax.broadcasted_iota(I32, (1, 128), 1).astype(F32)
    steps = lax.broadcasted_iota(I32, (tokens, 128), 0).astype(F32)
    for s in range(own):
        high, wide = high_at[s : s + 1, :], wide_at[s : s + 1, :]
        high, wide = jnp.maximum(high, 1.0), jnp.maximum(wide, 1.0)
        index = offset_at[s : s + 1, :].astype(F32) + steps
        frames = jnp.floor((index + 0.5) * (1.0 / (high * wide)))
        lines = jnp.floor((index + 0.5) * (1.0 / wide))
        place = jnp.where(
            lane_f < 32.0, frames,
            jnp.where(lane_f < 80.0, lines - high * frames + 32.0, index - wide * lines + 80.0),
        )
        hot = jnp.where(place == lane_f, 1.0, 0.0).astype(BF16)
        hot = jnp.concatenate([hot, hot], axis=1)
        cs[0, s] = jnp.dot(hot, halved[0], preferred_element_type=F32)
        cs[1, s] = jnp.dot(hot, halved[1], preferred_element_type=F32)

    for q in reversed(x_steps):
        at = xt.at[rem(x + heads - q // 2, heads) * 2 + (other if q % 2 else core)]
        pltpu.make_async_remote_copy(
            at, at, s3.at[q], r3.at[q], device_id=x_peer(q), device_id_type=MESH).wait_recv()
    for copy in sent:
        copy.wait_send()


def routed(
    across, clips, owners, slot_ids, latents, extents, we, be, shift, scale, gq, gk, wq, wk
):
    blocks, channels, tokens = latents.shape
    own = 2 * blocks
    heads, deep = lax.axis_size("head"), lax.axis_size("seq") // (2 * across)
    share, pair = channels // (2 * heads), tokens // 128
    both = 2 * own
    depth, columns = wq.shape
    chunks = 2 * columns // WIDE
    dma, room = pltpu.SemaphoreType.DMA, pltpu.VMEM
    table = jnp.asarray(rope_table())
    flat = [v.reshape(1, -1) for v in (be, gq, gk)]
    rows = own * (channels + 8)
    args = (clips, owners, slot_ids, latents, extents.T, we, flat[0], shift, scale, flat[1], flat[2], table, wq, wk)
    return pl.pallas_call(
        functools.partial(routing_kernel, deep=deep, across=across),
        out_shape=[
            jax.ShapeDtypeStruct((2 * heads, pair * own, share, 128), BF16),
            jax.ShapeDtypeStruct((chunks, own, 2, 2 * channels + 16, WIDE), BF16),
            jax.ShapeDtypeStruct((2, own, tokens, 256), F32),
            jax.ShapeDtypeStruct((3, channels + 16, channels + 16), BF16),
            jax.ShapeDtypeStruct((8, 128), F32),
        ],
        in_specs=[HBM] * len(args),
        out_specs=[VMEM] * 5,
        scratch_shapes=[
            pltpu.SMEM(clips.shape, I32), pltpu.SMEM(clips.shape, I32), pltpu.SMEM(clips.shape, I32),
            *(room(v.shape, v.dtype) for v in (args[4], we, flat[0], shift, scale, flat[1], flat[2], table)),
            room((chunks, depth, WIDE), BF16),
            room((rows, depth), BF16),
            room((2, rows, WIDE), F32),
            room((channels + 16, depth), F32),
            room((2, 256, 256), BF16),
            room((2, pair * blocks + 1, share, 128), BF16),
            room((2 * deep, pair * blocks + 1, share, 128), BF16),
            room((across, pair * both + 1, share, 128), BF16),
            room((across, both, share, 128), BF16),
            room((across, pair * both + 1, share, 128), BF16),
            room((2, pair * own, share, 128), BF16),
            dma((11 + 2 * pair,)), dma((chunks,)),
            dma((2 * deep,)), dma((2 * deep,)), dma((across,)), dma((across,)), dma((2 * heads,)), dma((2 * heads,)),
        ],
        compiler_params=pltpu.CompilerParams(
            collective_id=0, has_side_effects=True, vmem_limit_bytes=28 << 20),
        name="routing",
    )(*(pltpu.with_memory_space_constraint(v, pltpu.HBM) for v in args))


def finish_kernel(xt, stacks, cs, gram, use, oq, ok, zz, eps, out, o_sem):
    parts, both, share, _ = xt.shape
    slots, tokens = zz.shape[:2]
    pair = both // slots
    channels = parts * share
    chunks, _, _, deep, wide = stacks.shape
    per = chunks // 2
    sub = lax.broadcasted_iota(I32, (16, tokens), 0)
    e_row = lax.broadcasted_iota(I32, (deep, 128), 0)
    spread = jnp.where(e_row // 2 == channels + 3, 1.0, 0.0).astype(BF16)
    for s in range(slots):
        xf = jnp.concatenate(
            [jnp.concatenate([xt[p, h * slots + s].astype(F32) for h in range(pair)], axis=1)
             for p in range(parts)], axis=0)
        x1f = jnp.concatenate([xf, jnp.where(sub == 0, 1.0, 0.0)], axis=0)
        x1 = x1f.astype(BF16)
        y = sum(jnp.dot(gram[k], x1, preferred_element_type=F32) for k in range(3))
        var = jnp.maximum(jnp.sum(y * x1f, axis=0, keepdims=True), 0.0) + 1e-06
        dev = jnp.sqrt(var)
        dev_hi = dev.astype(BF16).astype(F32)
        small = var * (128.0 * 1e-06)
        small_hi = small.astype(BF16).astype(F32)
        live = jnp.concatenate([use[s : s + 1, :]] * (tokens // 128), axis=1)
        more = jnp.where((sub == 1) | (sub == 4), dev_hi, jnp.where(sub == 2, dev - dev_hi, 1.0)) * live
        more = jnp.where(sub < 5, more, jnp.where(sub == 6, small_hi, jnp.where(sub == 7, small - small_hi, 0.0)))
        zt = jnp.concatenate([xf, xf, more], axis=0)
        z = zt.astype(BF16).T
        eps[s] = jnp.dot(z, spread, preferred_element_type=F32)
        zz[s] = z

    def out_copy(n, s):
        place = oq if n < per else ok
        rows = pl.ds(s * tokens, tokens)
        return pltpu.make_async_copy(
            out.at[n, rows], place.at[rows, pl.ds(n % per * wide, wide)], o_sem.at[n, s])

    def chunk(n):
        for s in range(slots):
            z = zz[s]
            v = jnp.dot(z, stacks[n, s, 0], preferred_element_type=F32)
            vs = jnp.dot(z, stacks[n, s, 1], preferred_element_type=F32)
            c = cs[n // per, s, :, 0:128]
            sn = cs[n // per, s, :, 128:256]
            e = eps[s]
            for h in range(wide // 128):
                at = slice(h * 128, (h + 1) * 128)
                power = jnp.sum(v[:, at] * v[:, at], axis=1, keepdims=True)
                o = (v[:, at] * c + vs[:, at] * sn) * lax.rsqrt(power + e)
                out[n, s * tokens : (s + 1) * tokens, at] = o.astype(BF16)
            out_copy(n, s).start()

    for n in range(chunks):
        chunk(n)
    for n in range(chunks):
        for s in range(slots):
            out_copy(n, s).wait()


def finished(xt, stacks, cs, gram, use):
    slots, tokens = cs.shape[1:3]
    chunks, _, _, deep, wide = stacks.shape
    rows = slots * tokens
    return pl.pallas_call(
        finish_kernel,
        out_shape=[jax.ShapeDtypeStruct((rows, chunks // 2 * wide), BF16)] * 2,
        in_specs=[VMEM] * 5,
        out_specs=[pl.BlockSpec(memory_space=pl.ANY)] * 2,
        scratch_shapes=[
            pltpu.VMEM((slots, tokens, deep), BF16),
            pltpu.VMEM((slots, tokens, 128), F32),
            pltpu.VMEM((chunks, rows, wide), BF16),
            pltpu.SemaphoreType.DMA((chunks, slots)),
        ],
        compiler_params=pltpu.CompilerParams(vmem_limit_bytes=28 << 20),
        name="finish",
    )(xt, stacks, cs, gram, use)


def per_device(
    across, latents, clip_ids, owners, slots, extents, embed_weight, embed_bias, shift_table, scale_table,
    query_weight, key_weight, query_gain, key_gain,
):
    parts = routed(
        across, clip_ids, owners, slots, jnp.transpose(latents, (0, 2, 1)), extents, embed_weight, embed_bias,
        shift_table, scale_table, query_gain, key_gain, query_weight, key_weight,
    )
    return tuple(finished(*parts))


def solution(mesh):
    placed = (
        P("seq", None, None),
        P("seq"),
        P("seq"),
        P("seq"),
        P(),
        P(),
        P(),
        P(),
        P(),
        P(None, "head"),
        P(None, "head"),
        P(),
        P(),
    )
    return jax.shard_map(
        functools.partial(per_device, 4),
        mesh=mesh,
        in_specs=placed,
        out_specs=(P("seq", "head"), P("seq", "head")),
        check_vma=False,
    )
```
